256 devices in a mesh: gz: 4 (over x), grid: 64 (over y, z, core).
Axes of the slice: x: 4, y: 4, z: 8, core: 2. Of those that a mesh axis runs over, the one named last changes fastest.
Arguments:
- rhs: bfloat16 [6, 128, 32, 128], P(None, 'grid'), may hold values from -6 to 6
- lower_updates: bfloat16 [4, 6, 128, 32, 128], P('gz', None, 'grid'), may hold values from -6 to 6
- diag_inv: bfloat16 [6, 128, 128, 128], P(None, 'grid'), may hold values from -0.5 to 0.5
- lower_blocks: bfloat16 [5, 128, 128, 128], P(None, 'grid'), may hold values from -0.5 to 0.5
- upper_inv: bfloat16 [6, 128, 128, 128], P(None, 'grid'), may hold values from -0.5 to 0.5
- upper_blocks: bfloat16 [5, 128, 128, 128], P(None, 'grid'), may hold values from -0.5 to 0.5
- parent: int32 [5, 128], P(None, 'grid'), may hold values from 0 to 127, as said below
- live_count: int32 [6, 64], P(None, 'grid'), may hold values from 1 to 2
Outputs:
- solution: bfloat16 [6, 128, 32, 128], P(None, 'grid')
The draws below stay inside these ranges and needn't reach their ends.
Inputs may be any that keep to these rules, and one draw needn't show every extreme that they name: At level l the slots form aligned groups of S = min(128, 4 * 2 * 2 ** l) slots (those of min(64, 4 * 2 ** l) grid indices in a row); parent[l, g] lies in the group of g, between (g // S) * S and (g // S) * S + S - 1, and both ends are named in every group.
All inputs are finite; a program needn't handle non-finite values.
Results may differ from the reference program's by a relative error of at most 0.03.
Values may be sent and summed in bfloat16 or wider, within the bound.
A program may use at most 64 MiB of HBM per device.

```python
import jax
import jax.numpy as jnp

W = 128
R = 32
LEV = 6
SL = 2
NBS = 128
N_GZ = 4
N_GRID = 64


def draw_parent(key, part):
    level_ids = jnp.arange(LEV - 1, dtype=jnp.int32)[:, None]
    slot_ids = jnp.arange(NBS, dtype=jnp.int32)[None, :]
    group = jnp.minimum(NBS, 4 * SL * jnp.power(2, level_ids)).astype(jnp.int32)
    base = slot_ids // group * group
    position = slot_ids - base
    first_key = jax.random.fold_in(key, 11)
    second_key = jax.random.fold_in(key, 23)
    first_pick = jax.random.randint(first_key, (LEV - 1, NBS), 0, 1 << 30, dtype=jnp.int32) % group
    second_pick = jax.random.randint(second_key, (LEV - 1, NBS), 0, 1 << 30, dtype=jnp.int32) % group
    picked = jnp.minimum(first_pick, second_pick)
    picked = jnp.where(position == group - 1, group - 1, jnp.where(position == 0, 0, picked))
    return (base + picked).astype(jnp.int32)


def set_ends(values, stream_key, smallest, high):
    longest = values.shape.index(max(values.shape))
    spots = []
    for shift in (0, 1):
        where = [jax.random.randint(jax.random.fold_in(stream_key, axis), (), 0, length) for axis, length in enumerate(values.shape)]
        where[longest] = (where[longest] + shift) % values.shape[longest]
        spots.append(tuple(where))
    return values.at[spots[0]].set(smallest).at[spots[1]].set(high)


def steps_of(own_key, extent, cuts, least, top_value):
    gain = 1.0
    for dim, shards_of in cuts:
        steps = jax.random.uniform(jax.random.fold_in(jax.random.fold_in(own_key, 6), dim), (shards_of,), jnp.float32, least / len(cuts), top_value / len(cuts))
        gain = gain * jnp.repeat(jnp.exp(steps), extent[dim] // shards_of).reshape((-1,) + (1,) * (len(extent) - 1 - dim))
    return gain


def gaussian(rng, shape, width, most, cuts=(), kind=jnp.bfloat16):
    loudness = steps_of(rng, shape, cuts, -0.22, 0.18) if cuts else 1.0
    drawn = jax.random.normal(rng, shape, jnp.float32) * width * loudness
    return jnp.minimum(jnp.maximum(drawn, -most), most).astype(kind)


def setup_inputs(seed: int = 0) -> dict:
    streams_of = jax.random.split(jax.random.key(seed), 9)
    return {
        "rhs": gaussian(streams_of[0], (LEV, NBS, R, W), 1.0, 6.0, ((1, 64),)),
        "lower_updates": gaussian(streams_of[1], (N_GZ, LEV, NBS, R, W), 0.5, 6.0, ((0, 4), (2, 64))),
        "diag_inv": gaussian(streams_of[2], (LEV, NBS, W, W), W ** -0.5, 0.5, ((1, 64),)),
        "lower_blocks": gaussian(streams_of[3], (LEV - 1, NBS, W, W), W ** -0.5, 0.5, ((1, 64),)),
        "upper_inv": gaussian(streams_of[4], (LEV, NBS, W, W), W ** -0.5, 0.5, ((1, 64),)),
        "upper_blocks": gaussian(streams_of[5], (LEV - 1, NBS, W, W), W ** -0.5, 0.5, ((1, 64),)),
        "parent": draw_parent(jax.random.fold_in(streams_of[8], 71), 0),
        "live_count": set_ends(jax.random.randint(streams_of[7], (LEV, N_GRID), 1, SL + 1), jax.random.fold_in(streams_of[7], 1), 1, SL).astype(jnp.int32),
    }


def reference(rhs, lower_updates, diag_inv, lower_blocks, upper_inv, upper_blocks, parent, live_count):
    f32 = jnp.float32
    bf16 = jnp.bfloat16
    index = jnp.arange(NBS, dtype=jnp.int32)
    owner = index // SL
    slot = index % SL
    live = (slot[None, :] < live_count[:, owner]).astype(f32)
    updates = jnp.sum(lower_updates.astype(f32), axis=0)
    incoming = jnp.zeros((NBS, R, W), f32)
    forward_all = []
    for level in range(LEV):
        residual = (rhs[level].astype(f32) - updates[level] - incoming).astype(bf16)
        forward = jnp.einsum('grw,gwv->grv', residual.astype(f32), diag_inv[level].astype(f32))
        forward = (forward * live[level][:, None, None]).astype(bf16)
        forward_all.append(forward)
        if level + 1 < LEV:
            sent = jnp.einsum('grw,gwv->grv', forward.astype(f32), lower_blocks[level].astype(f32)).astype(bf16)
            incoming = jax.ops.segment_sum(sent.astype(f32), parent[level], num_segments=NBS)
    answer = [None] * LEV
    for level in range(LEV - 1, -1, -1):
        if level == LEV - 1:
            target = forward_all[level].astype(f32)
        else:
            above = answer[level + 1][parent[level]]
            target = forward_all[level].astype(f32) - jnp.einsum('grw,gwv->grv', above.astype(f32), upper_blocks[level].astype(f32))
        target = target.astype(bf16)
        result = jnp.einsum('grw,gwv->grv', target.astype(f32), upper_inv[level].astype(f32))
        answer[level] = (result * live[level][:, None, None]).astype(bf16)
    return jnp.stack(answer)
```

```python
import functools

import jax
import jax.numpy as jnp
from jax import lax
from jax.experimental import pallas as pl
from jax.experimental.pallas import tpu as pltpu
from jax.sharding import PartitionSpec as P

MESH = pl.DeviceIdType.MESH
F32 = jnp.float32
BF16 = jnp.bfloat16


def kernel(
    nx,
    ng,
    parent,
    live_count,
    rhs,
    upd,
    diag_hbm,
    lower_hbm,
    vinv_hbm,
    upper_hbm,
    out,
    diag,
    lower,
    vinv,
    upper,
    ml,
    uv,
    rhs_own,
    upd_all,
    fv,
    sol,
    build,
    up_in,
    downs,
    load_sem,
    rs_send,
    rs_recv,
    up_send,
    up_recv,
    down_send,
    down_recv,
    ag_send,
    ag_recv,
    own_sem,
):
    levels = rhs.shape[0]
    x = lax.axis_index("gz")
    g = lax.axis_index("grid")
    sizes = [min(ng, 4 * 2**l) for l in range(levels - 1)]

    barrier = pltpu.get_barrier_semaphore()

    def greet(j, c):
        other = lax.rem(g + 1 + j, ng)
        pl.semaphore_signal(barrier, inc=1, device_id=(x, other), device_id_type=MESH)
        return c

    lax.fori_loop(0, ng - 1, greet, 0)
    for k in range(1, nx):
        pl.semaphore_signal(
            barrier, inc=1, device_id=(lax.rem(x + k, nx), g), device_id_type=MESH
        )

    loads = [
        pltpu.make_async_copy(rhs.at[:, :, x], rhs_own, load_sem.at[0]),
        pltpu.make_async_copy(upd.at[:, :, x], upd_all.at[0], load_sem.at[1]),
        pltpu.make_async_copy(diag_hbm, diag, load_sem.at[2]),
        pltpu.make_async_copy(lower_hbm, lower, load_sem.at[3]),
        pltpu.make_async_copy(vinv_hbm, vinv, load_sem.at[4]),
        pltpu.make_async_copy(upper_hbm, upper, load_sem.at[5]),
    ]
    for c in loads:
        c.start()

    pl.semaphore_wait(barrier, ng - 1 + nx - 1)

    def rs_copies(part):
        span = pl.ds(0, 1) if part == 0 else pl.ds(1, levels - 1)
        return [
            pltpu.make_async_remote_copy(
                src_ref=upd.at[span, :, lax.rem(x + k, nx)],
                dst_ref=upd_all.at[k, span],
                send_sem=rs_send.at[k - 1, part],
                recv_sem=rs_recv.at[k - 1, part],
                device_id=(lax.rem(x + k, nx), g),
                device_id_type=MESH,
            )
            for k in range(1, nx)
        ]

    rs = [rs_copies(0), rs_copies(1)]
    for part in rs:
        for c in part:
            c.start()

    loads[2].wait()
    loads[3].wait()

    def products(a, b, dst, l):
        for s in range(2):
            m = jnp.dot(a[l, s], b[l, s], preferred_element_type=F32)
            dst[l, pl.ds(128 * s, 128), :] = m.astype(BF16)

    products(diag, lower, ml, 0)
    loads[4].wait()
    loads[5].wait()
    loads[0].wait()
    loads[1].wait()

    row = lax.broadcasted_iota(jnp.int32, (16, 128), 0)
    second = row >= 8
    slotrow = row // 8

    def spread(v):
        zero = jnp.zeros_like(v)
        return jnp.concatenate(
            [jnp.where(second, zero, v), jnp.where(second, v, zero)], axis=1
        ).astype(BF16)

    def live_of(l):
        return (slotrow < live_count[l, 0]).astype(F32)

    def mats(ref, l):
        return ref[l].reshape(256, 128)

    for c in rs[0]:
        c.wait_recv()

    incoming = None
    for l in range(levels):
        if l == 1:
            for c in rs[1]:
                c.wait_recv()
        total = rhs_own[l].astype(F32).reshape(16, 128)
        for k in range(nx):
            total = total - upd_all[k, l].astype(F32).reshape(16, 128)
        if incoming is not None:
            total = total - incoming
        live = live_of(l)
        res = spread(total)
        if l == levels - 1:
            fwd = jnp.dot(res, mats(diag, l), preferred_element_type=F32) * live
            top = jnp.dot(spread(fwd), mats(vinv, l), preferred_element_type=F32)
            sol[l] = (top * live).astype(BF16)
            break
        n = sizes[l]
        rel = lax.rem(g, n)
        base = g - rel
        sent = jnp.dot(res, ml[l], preferred_element_type=F32) * live
        a = jnp.concatenate([sent[:8], sent[:8]], axis=0)
        b = jnp.concatenate([sent[8:], sent[8:]], axis=0)
        pa = parent[l, 0] - 2 * base - slotrow
        pb = parent[l, 1] - 2 * base - slotrow
        zero = jnp.zeros_like(a)

        def tile(d):
            return (
                jnp.where(pa == 2 * d, a, zero) + jnp.where(pb == 2 * d, b, zero)
            ).astype(BF16)

        offset = sum(sizes[:l])
        for d in range(n):
            build[offset + d] = tile(d)
        own = tile(rel)

        def start(j, c, l=l, n=n, rel=rel, base=base, offset=offset):
            k = n // 2 + (1 - 2 * lax.rem(j, 2)) * ((j + 1) // 2)
            dest = lax.rem(rel + k, n)
            pltpu.make_async_remote_copy(
                src_ref=build.at[offset + dest],
                dst_ref=up_in.at[offset + k],
                send_sem=up_send.at[l],
                recv_sem=up_recv.at[l],
                device_id=(x, base + dest),
                device_id_type=MESH,
            ).start()
            return c

        lax.fori_loop(0, n - 1, start, 0)

        fwd = jnp.dot(res, mats(diag, l), preferred_element_type=F32) * live
        fv[l] = jnp.dot(spread(fwd), mats(vinv, l), preferred_element_type=F32)
        if l + 1 < levels - 1:
            products(diag, lower, ml, l + 1)
        products(upper, vinv, uv, l)

        whole = up_in.at[pl.ds(offset + 1, n - 1)]
        pltpu.make_async_copy(whole, whole, up_recv.at[l]).wait()
        incoming = own.astype(F32)
        for k in range(1, n):
            incoming = incoming + up_in[offset + k].astype(F32)

    def share(l):
        for k in range(1, nx):
            pltpu.make_async_remote_copy(
                src_ref=sol.at[l],
                dst_ref=out.at[l, x],
                send_sem=ag_send.at[0],
                recv_sem=ag_recv.at[0],
                device_id=(lax.rem(x + k, nx), g),
                device_id_type=MESH,
            ).start()
        pltpu.make_async_copy(sol.at[l], out.at[l, x], own_sem.at[l]).start()

    for l in range(levels - 2, -1, -1):
        n = sizes[l]
        rel = lax.rem(g, n)
        base = g - rel

        def start(j, c, l=l, n=n, rel=rel, base=base):
            k = n // 2 + (1 - 2 * lax.rem(j, 2)) * ((j + 1) // 2)
            dest = lax.rem(rel + k, n)
            pltpu.make_async_remote_copy(
                src_ref=sol.at[l + 1],
                dst_ref=downs[l].at[rel],
                send_sem=down_send.at[l],
                recv_sem=down_recv.at[l],
                device_id=(x, base + dest),
                device_id_type=MESH,
            ).start()
            return c

        lax.fori_loop(0, n - 1, start, 0)
        downs[l][rel] = sol[l + 1]
        share(l + 1)
        whole = downs[l].at[pl.ds(0, n - 1)]
        pltpu.make_async_copy(whole, whole, down_recv.at[l]).wait()
        picked = []
        for s in range(2):
            p = lax.rem(parent[l, s], 2 * n)
            t = downs[l][p // 2].astype(F32)
            picked.append(jnp.where(lax.rem(p, 2) == 0, t[:8], t[8:]))
        above = jnp.concatenate(picked, axis=0)
        low = jnp.dot(spread(above), uv[l], preferred_element_type=F32)
        sol[l] = ((fv[l] - low) * live_of(l)).astype(BF16)
    share(0)

    for part in rs:
        for c in part:
            c.wait_send()
    for l in range(levels - 1):
        n = sizes[l]
        offset = sum(sizes[:l])
        whole = up_in.at[pl.ds(offset, n - 1)]
        pltpu.make_async_copy(whole, whole, up_send.at[l]).wait()
        pltpu.make_async_copy(whole, whole, down_send.at[l]).wait()
    for l in range(levels):
        pltpu.make_async_copy(sol.at[l], out.at[l, x], own_sem.at[l]).wait()
    whole = out.at[:, pl.ds(0, nx - 1)]
    pltpu.make_async_copy(whole, whole, ag_send.at[0]).wait()
    pltpu.make_async_copy(whole, whole, ag_recv.at[0]).wait()


def solution(mesh):
    nx, ng = mesh.shape["gz"], mesh.shape["grid"]

    def on_device(rhs, upd, diag, lower, vinv, upper, parent, live_count):
        levels, slots, rows, width = rhs.shape
        part = rows // nx
        hbm = pl.BlockSpec(memory_space=pl.ANY)
        smem = pl.BlockSpec(memory_space=pltpu.SMEM)
        total = sum(min(ng, 4 * 2**l) for l in range(levels - 1))
        dma = pltpu.SemaphoreType.DMA
        result = pl.pallas_call(
            functools.partial(kernel, nx, ng),
            out_shape=jax.ShapeDtypeStruct((levels, nx, slots * part, width), BF16),
            in_specs=[smem, smem] + [hbm] * 6,
            out_specs=hbm,
            scratch_shapes=[
                pltpu.VMEM(diag.shape, BF16),
                pltpu.VMEM(lower.shape, BF16),
                pltpu.VMEM(vinv.shape, BF16),
                pltpu.VMEM(upper.shape, BF16),
                pltpu.VMEM((levels - 1, slots * width, width), BF16),
                pltpu.VMEM((levels - 1, slots * width, width), BF16),
                pltpu.VMEM((levels, slots, part, width), BF16),
                pltpu.VMEM((nx, levels, slots, part, width), BF16),
                pltpu.VMEM((levels - 1, slots * part, width), F32),
                pltpu.VMEM((levels, slots * part, width), BF16),
                pltpu.VMEM((total, slots * part, width), BF16),
                pltpu.VMEM((total, slots * part, width), BF16),
                [
                    pltpu.VMEM((min(ng, 4 * 2**l), slots * part, width), BF16)
                    for l in range(levels - 1)
                ],
                dma((6,)),
                dma((nx - 1, 2)),
                dma((nx - 1, 2)),
                dma((levels - 1,)),
                dma((levels - 1,)),
                dma((levels - 1,)),
                dma((levels - 1,)),
                dma((1,)),
                dma((1,)),
                dma((levels,)),
            ],
            compiler_params=pltpu.CompilerParams(
                collective_id=0, has_side_effects=True
            ),
        )(
            parent,
            live_count,
            rhs.reshape(levels, slots, nx, part, width),
            upd.reshape(levels, slots, nx, part, width),
            diag,
            lower,
            vinv,
            upper,
        )
        result = result.reshape(levels, nx, slots, part, width)
        return result.transpose(0, 2, 1, 3, 4).reshape(rhs.shape)

    return jax.shard_map(
        on_device,
        mesh=mesh,
        in_specs=(
            P(None, "grid", None, None),
            P("gz", None, "grid", None, None),
            P(None, "grid", None, None),
            P(None, "grid", None, None),
            P(None, "grid", None, None),
            P(None, "grid", None, None),
            P(None, "grid"),
            P(None, "grid"),
        ),
        out_specs=P(None, "grid", None, None),
        check_vma=False,
    )
```

```python
import functools

import jax
import jax.numpy as jnp
from jax import lax
from jax.experimental import pallas as pl
from jax.experimental.pallas import tpu as pltpu
from jax.sharding import PartitionSpec as P

MESH = pl.DeviceIdType.MESH
F32 = jnp.float32
BF16 = jnp.bfloat16
NX, NY, NZ, NC = 4, 4, 8, 2
LEVELS = 6
CHIPS_Z = (2, 4, 8, 8, 8)
CHIPS_Y = (1, 1, 1, 2, 4)
SIZES = tuple(NC * a * b for a, b in zip(CHIPS_Z, CHIPS_Y))


def ring(k, n):
    return min(k, n - k)


def offsets(mz, my, cores):
    every = [
        (dy, dz, dc) for dy in range(my) for dz in range(mz) for dc in range(cores)
    ]
    every.sort(key=lambda o: -(ring(o[0], NY) + ring(o[1], NZ)))
    return [o for o in every if o != (0, 0, 0)]


def kernel(
    parent,
    live_count,
    rhs,
    upd,
    diag_hbm,
    lower_hbm,
    vinv_hbm,
    upper_hbm,
    out,
    diag,
    lower,
    vinv,
    upper,
    ml,
    uv_own,
    uv_part,
    tabs,
    ftabs,
    ids_own,
    ids,
    rhs_own,
    rhs_first,
    upd_first,
    upd_all,
    fv,
    sol,
    chain,
    build,
    build0,
    in0,
    ins,
    mate,
    top_tab,
    mid_tab,
    load_sem,
    send,
    recv,
    rs_send,
    rs_recv,
    tab_send,
    tab_recv,
    f_send,
    f_recv,
    own_sem,
):
    x = lax.axis_index("gz")
    g = lax.axis_index("grid")
    y, z, c = g // (NZ * NC), lax.rem(g // NC, NZ), lax.rem(g, NC)

    zs = {m: [z // m * m + lax.rem(z + k, m) for k in range(m)] for m in (2, 4, 8)}
    ys = {m: [y // m * m + lax.rem(y + k, m) for k in range(m)] for m in (1, 2, 4)}
    cs = [c, 1 - c]
    xs = [lax.rem(x + k, NX) for k in range(NX)]

    def at(off, mz, my):
        dy, dz, dc = off
        return (ys[my][dy] * NZ + zs[mz][dz]) * NC + cs[dc]

    def remote(src, dst, s, r, gx, gg):
        return pltpu.make_async_remote_copy(
            src_ref=src,
            dst_ref=dst,
            send_sem=s,
            recv_sem=r,
            device_id=(gx, gg),
            device_id_type=MESH,
        )

    def wait(view, sem):
        pltpu.make_async_copy(view, view, sem).wait()

    barrier = pltpu.get_barrier_semaphore()
    near = [(k, g) for k in xs[1:]]
    near += [(k, at(o, 2, 1)) for k in xs for o in offsets(2, 1, 2)]
    near += [(x, at((dy, 0, 0), 8, 4)) for dy in (1, 3)]
    far = [(0, dz, dc) for dz in (1, 2, 6, 7) for dc in (0, 1)]
    for gx, gg in near:
        pl.semaphore_signal(barrier, inc=1, device_id=(gx, gg), device_id_type=MESH)
    for o in far:
        pl.semaphore_signal(
            barrier, inc=1, device_id=(x, at(o, 8, 4)), device_id_type=MESH
        )

    loads = [
        pltpu.make_async_copy(upd.at[0], upd_first, load_sem.at[0]),
        pltpu.make_async_copy(rhs.at[0], rhs_first, load_sem.at[1]),
        pltpu.make_async_copy(diag_hbm, diag, load_sem.at[2]),
        pltpu.make_async_copy(lower_hbm, lower, load_sem.at[3]),
        pltpu.make_async_copy(vinv_hbm, vinv, load_sem.at[4]),
        pltpu.make_async_copy(upper_hbm, upper, load_sem.at[5]),
        pltpu.make_async_copy(rhs.at[:, :, x], rhs_own, load_sem.at[6]),
        pltpu.make_async_copy(upd.at[:, :, x], upd_all.at[0], load_sem.at[7]),
    ]
    for copy in loads:
        copy.start()
    for l in range(LEVELS - 1):
        for s in range(2):
            ids_own[0, 2 * l + s] = parent[s, l]

    row = lax.broadcasted_iota(jnp.int32, (16, 128), 0)
    slotrow = row // 8

    def spread(v, half):
        rows = lax.broadcasted_iota(jnp.int32, v.shape, 0)
        zero = jnp.zeros_like(v)
        return jnp.concatenate(
            [jnp.where(rows < half, v, zero), jnp.where(rows < half, zero, v)], axis=1
        ).astype(BF16)

    def live_of(l, rows=16):
        slot = lax.broadcasted_iota(jnp.int32, (rows, 128), 0) // (rows // 2)
        return (slot < live_count[0, l]).astype(F32)

    def dot(a, b):
        return jnp.dot(a, b, preferred_element_type=F32)

    def mats(ref, l):
        return ref[l].reshape(256, 128)

    def twice(v):
        return jnp.concatenate([v, v], axis=0)

    def target(p, n):
        return lax.rem(p, 2 * n) - slotrow

    def product(a, b, dst, l, place=None):
        for s in range(2):
            dst[l if place is None else place, pl.ds(128 * s, 128), :] = dot(
                a[l, s], b[l, s]
            ).astype(BF16)

    for k in range(4):
        loads[k].wait()
    first = rhs_first[...].astype(F32).reshape(64, 128) * (x == 0).astype(F32)
    first = first - upd_first[...].astype(F32).reshape(64, 128)
    f0 = dot(spread(first, 32), mats(diag, 0)) * live_of(0, 64)
    sent = dot(spread(f0, 32), mats(lower, 0))
    off0 = [(0, 0, 0)] + offsets(2, 1, 2)
    rels = [lax.rem(at(o, 2, 1), 4) for o in off0]
    pa, pb = target(parent[0, 0], 4), target(parent[1, 0], 4)
    for q in range(NX):
        a = twice(sent[8 * q : 8 * q + 8])
        b = twice(sent[32 + 8 * q : 40 + 8 * q])
        zero = jnp.zeros_like(a)
        for k, rel in enumerate(rels):
            build0[q, k] = (
                jnp.where(pa == 2 * rel, a, zero) + jnp.where(pb == 2 * rel, b, zero)
            ).astype(BF16)

    pl.semaphore_wait(barrier, len(near) + len(far))

    for dx in (2, 1, 3, 0):
        for k, o in enumerate(off0):
            if dx or k:
                remote(
                    build0.at[xs[dx], k],
                    in0.at[4 * dx + k],
                    send.at[0],
                    recv.at[0],
                    xs[dx],
                    at(o, 2, 1),
                ).start()
    rs = [
        remote(
            upd.at[:, :, xs[k]],
            upd_all.at[k],
            rs_send.at[k - 1],
            rs_recv.at[k - 1],
            xs[k],
            g,
        )
        for k in range(1, NX)
    ]
    for copy in rs:
        copy.start()

    for k in range(4, 8):
        loads[k].wait()
    part = pl.ds(32 * x, 32)
    for l in (1, 2, 3):
        for s in range(2):
            live = (s < live_count[0, l]).astype(F32)
            uv_part[l - 1, s] = (dot(upper[l, s, part, :], vinv[l, s]) * live).astype(
                BF16
            )

    def tab_first(l):
        nz = CHIPS_Z[l - 1]
        mine = lax.rem(z, nz)
        tab = tabs[l - 1]
        for o in offsets(nz, 1, 1):
            remote(
                uv_part.at[l - 1],
                tab.at[mine, c, :, x],
                tab_send.at[0, l - 1],
                tab_recv.at[0, l - 1],
                x,
                at(o, nz, 1),
            ).start()
        tab[mine, c, :, x] = uv_part[l - 1]

    def tab_first_wait(l):
        nz = CHIPS_Z[l - 1]
        wait(tabs[l - 1].at[pl.ds(0, nz - 1), 0, :, 0], tab_recv.at[0, l - 1])

    def tab_second(l):
        tab = tabs[l - 1]
        for k in (2, 1, 3):
            remote(
                tab.at[:, c, :, x],
                tab.at[:, c, :, x],
                tab_send.at[1, l - 1],
                tab_recv.at[1, l - 1],
                xs[k],
                g,
            ).start()

    def tab_second_wait(l):
        wait(tabs[l - 1].at[:, 0, :, pl.ds(0, NX - 1)], tab_recv.at[1, l - 1])

    def tab_third(l):
        tab = tabs[l - 1]
        remote(
            tab.at[:, c],
            tab.at[:, c],
            tab_send.at[2, l - 1],
            tab_recv.at[2, l - 1],
            x,
            at((0, 0, 1), 2, 1),
        ).start()

    def tab_third_wait(l):
        wait(tabs[l - 1].at[:, 0], tab_recv.at[2, l - 1])

    def f_share(l):
        n, nz = SIZES[l - 1], CHIPS_Z[l - 1]
        mine = lax.rem(g, n)
        tile = fv[l].astype(BF16)
        ftabs[l - 1][mine] = tile
        for o in offsets(nz, 1, 2):
            remote(
                ftabs[l - 1].at[mine],
                ftabs[l - 1].at[mine],
                f_send.at[l - 1],
                f_recv.at[l - 1],
                x,
                at(o, nz, 1),
            ).start()

    def forward(l, total):
        fwd = dot(spread(total, 8), mats(diag, l)) * live_of(l)
        fv[l] = dot(spread(fwd, 8), mats(vinv, l)) * live_of(l)

    def base(l):
        total = rhs_own[l].astype(F32).reshape(16, 128)
        for k in range(NX):
            total = total - upd_all[k, l].astype(F32).reshape(16, 128)
        return total

    product(diag, lower, ml, 1)
    tab_first(1)
    for copy in rs:
        copy.wait_recv()
    bases = base(1)
    wait(in0.at[pl.ds(1, 15)], recv.at[0])
    incoming = build0[x, 0].astype(F32)
    for k in range(1, 16):
        incoming = incoming + in0[k].astype(F32)

    for l in (1, 2, 3):
        n, mz, my = SIZES[l], CHIPS_Z[l], CHIPS_Y[l]
        total = bases - incoming
        sent = dot(spread(total, 8), ml[l]) * live_of(l)
        a, b = twice(sent[:8]), twice(sent[8:])
        zero = jnp.zeros_like(a)
        pa, pb = target(parent[0, l], n), target(parent[1, l], n)

        def tile(rel):
            return (
                jnp.where(pa == 2 * rel, a, zero) + jnp.where(pb == 2 * rel, b, zero)
            ).astype(BF16)

        offs = offsets(mz, my, 2)
        goals = [at(o, mz, my) for o in offs]
        start = sum(SIZES[1:l])
        for k, goal in enumerate(goals):
            build[start + k] = tile(lax.rem(goal, n))
        for k, goal in enumerate(goals):
            remote(
                build.at[start + k], ins[l - 1].at[k], send.at[l], recv.at[l], x, goal
            ).start()
        own = tile(lax.rem(g, n)).astype(F32)

        forward(l, total)
        f_share(l)
        product(diag, lower, ml, l + 1)
        if l == 1:
            tab_first(2)
            forward(0, base(0))
        if l == 2:
            tab_first(3)
            mine = lax.rem(g, 16)
            for s in range(10):
                ids[mine, s] = ids_own[0, s]
            for o in offsets(8, 1, 2):
                remote(
                    ids_own,
                    ids.at[pl.ds(mine, 1)],
                    send.at[8],
                    recv.at[8],
                    x,
                    at(o, 8, 1),
                ).start()
        if l == 3:
            for j in (1, 2, 3):
                tab_first_wait(j)
                tab_second(j)
            product(upper, vinv, uv_own, 0)
        bases = base(l + 1)
        wait(ins[l - 1].at[pl.ds(0, n - 1)], recv.at[l])
        incoming = own
        for k in range(n - 1):
            incoming = incoming + ins[l - 1][k].astype(F32)

    total = bases - incoming
    sent = dot(spread(total, 8), ml[4]) * live_of(4)
    partner = at((0, 0, 1), 2, 1)
    mate[0] = sent.astype(BF16)
    remote(mate.at[0], mate.at[1], send.at[5], recv.at[5], x, partner).start()
    wait(ids.at[pl.ds(0, 15)], recv.at[8])
    pa, pb = target(parent[0, 4], 64), target(parent[1, 4], 64)
    other = lax.rem(partner, 16)
    pc, pd = target(ids[other, 8], 64), target(ids[other, 9], 64)
    offs = offsets(8, 4, 1)
    goals = [at(o, 8, 4) for o in offs]
    a, b = twice(sent[:8]), twice(sent[8:])
    bases = base(5)
    wait(mate.at[1], recv.at[5])
    third = mate[1].astype(F32)
    d, e = twice(third[:8]), twice(third[8:])
    zero = jnp.zeros_like(a)

    def tile4(goal):
        return (
            jnp.where(pa == 2 * goal, a, zero)
            + jnp.where(pb == 2 * goal, b, zero)
            + jnp.where(pc == 2 * goal, d, zero)
            + jnp.where(pd == 2 * goal, e, zero)
        ).astype(BF16)

    start = sum(SIZES[1:4])
    for k, goal in enumerate(goals):
        build[start + k] = tile4(goal)
    for k, goal in enumerate(goals):
        remote(
            build.at[start + k], ins[3].at[k], send.at[4], recv.at[4], x, goal
        ).start()
    own = tile4(g).astype(F32)
    forward(4, total)
    product(upper, vinv, uv_own, 4, 1)
    for j in (1, 2, 3):
        tab_second_wait(j)
        tab_third(j)
    wait(ins[3].at[pl.ds(0, 31)], recv.at[4])
    incoming = own
    for k in range(31):
        incoming = incoming + ins[3][k].astype(F32)

    fwd = dot(spread(bases - incoming, 8), mats(diag, 5)) * live_of(5)
    sol[5] = (dot(spread(fwd, 8), mats(vinv, 5)) * live_of(5)).astype(BF16)

    def share(first, count):
        span = pl.ds(first, count)
        for k in (2, 1, 3):
            remote(
                sol.at[span], out.at[span, x], send.at[9], recv.at[9], xs[k], g
            ).start()
        pltpu.make_async_copy(
            sol.at[span], out.at[span, x], own_sem.at[first]
        ).start()

    def half(t, p):
        t = t.astype(F32)
        return jnp.where(lax.rem(p, 2) == 0, t[:8], t[8:])

    chip = y * NZ + z
    for o in offs:
        remote(
            sol.at[5], top_tab.at[chip, c], send.at[6], recv.at[6], x, at(o, 8, 4)
        ).start()
    top_tab[chip, c] = sol[5]
    share(5, 1)

    for j in (1, 2, 3):
        tab_third_wait(j)
        wait(ftabs[j - 1].at[pl.ds(0, SIZES[j - 1] - 1)], f_recv.at[j - 1])

    def tab_mat(l, p):
        return tabs[l - 1][p // 4, lax.rem(p // 2, 2), lax.rem(p, 2)].reshape(128, 128)

    ancestors = [[None, None] for _ in range(4)]
    for k in range(4):
        consts = []
        for s in range(2):
            own_p = [lax.rem(2 * g + s, 2 * SIZES[j - 1]) for j in range(1, 4)]
            path = {}
            p = parent[s, k]
            for j in range(k + 1, 4):
                n = SIZES[j - 1]
                q = lax.rem(p, 2 * n)
                path[j] = q
                p = ids[lax.rem(p // 2, 16), 2 * j + lax.rem(p, 2)]
            ancestors[k][s] = lax.rem(p, 64)
            if k > 0:
                path[k] = own_p[k - 1]
            m = const = None
            for j in range(3, k - 1, -1):
                if j == 0:
                    u = uv_own[0, pl.ds(128 * s, 128), :]
                else:
                    u = tab_mat(j, path[j])
                if j == k:
                    f = fv[k][8 * s : 8 * s + 8]
                else:
                    f = half(ftabs[j - 1][path[j] // 2], path[j])
                if m is None:
                    m, const = u, f
                else:
                    const = f - dot(const.astype(BF16), u)
                    m = dot(m, u).astype(BF16)
            chain[k, pl.ds(128 * s, 128), :] = m
            consts.append(const)
        fv[k] = jnp.concatenate(consts, axis=0)

    wait(top_tab.at[pl.ds(0, 31), 0], recv.at[6])
    remote(
        top_tab.at[:, c], top_tab.at[:, c], send.at[7], recv.at[7], x, partner
    ).start()
    wait(top_tab.at[:, 0], recv.at[7])
    above = jnp.concatenate(
        [
            half(top_tab[p // 4, lax.rem(p // 2, 2)], p)
            for p in (lax.rem(parent[0, 4], 128), lax.rem(parent[1, 4], 128))
        ],
        axis=0,
    )
    low = dot(spread(above, 8), uv_own[1])
    sol[4] = ((fv[4] - low) * live_of(4)).astype(BF16)

    mine = lax.rem(g, 32)
    offs = offsets(8, 2, 2)
    for o in offs:
        remote(
            sol.at[4], mid_tab.at[mine], send.at[10], recv.at[10], x, at(o, 8, 2)
        ).start()
    mid_tab[mine] = sol[4]
    share(4, 1)
    wait(mid_tab.at[pl.ds(0, 31)], recv.at[10])
    for k in range(4):
        above = jnp.concatenate(
            [half(mid_tab[p // 2], p) for p in ancestors[k]], axis=0
        )
        low = dot(spread(above, 8), chain[k])
        value = fv[k] - low if k % 2 == 1 else fv[k] + low
        sol[k] = (value * live_of(k)).astype(BF16)
    share(0, 4)

    wait(in0.at[pl.ds(1, 15)], send.at[0])
    for copy in rs:
        copy.wait_send()
    for l in (1, 2, 3):
        wait(ins[l - 1].at[pl.ds(0, SIZES[l] - 1)], send.at[l])
        nz = CHIPS_Z[l - 1]
        wait(tabs[l - 1].at[pl.ds(0, nz - 1), 0, :, 0], tab_send.at[0, l - 1])
        wait(tabs[l - 1].at[:, 0, :, pl.ds(0, NX - 1)], tab_send.at[1, l - 1])
        wait(tabs[l - 1].at[:, 0], tab_send.at[2, l - 1])
        wait(ftabs[l - 1].at[pl.ds(0, SIZES[l - 1] - 1)], f_send.at[l - 1])
    wait(ins[3].at[pl.ds(0, 31)], send.at[4])
    wait(mate.at[0], send.at[5])
    wait(top_tab.at[pl.ds(0, 31), 0], send.at[6])
    wait(top_tab.at[:, 0], send.at[7])
    wait(ids.at[pl.ds(0, 15)], send.at[8])
    wait(mid_tab.at[pl.ds(0, 31)], send.at[10])
    for first, count in ((5, 1), (4, 1), (0, 4)):
        span = pl.ds(first, count)
        pltpu.make_async_copy(
            sol.at[span], out.at[span, x], own_sem.at[first]
        ).wait()
    whole = out.at[:, pl.ds(0, NX - 1)]
    wait(whole, send.at[9])
    wait(whole, recv.at[9])


def solution(mesh):
    def on_device(rhs, upd, diag, lower, vinv, upper, parent, live_count):
        levels, slots, rows, width = rhs.shape
        part = rows // NX
        hbm = pl.BlockSpec(memory_space=pl.ANY)
        smem = pl.BlockSpec(memory_space=pltpu.SMEM)
        dma = pltpu.SemaphoreType.DMA
        pair = slots * width
        tile = (slots * part, width)
        split = (slots, NX, part, width)

        def vmem(*shape, dtype=BF16):
            return pltpu.VMEM(shape, dtype)

        result = pl.pallas_call(
            kernel,
            out_shape=jax.ShapeDtypeStruct((levels, NX) + tile, BF16),
            in_specs=[smem, smem] + [hbm] * 6,
            out_specs=hbm,
            scratch_shapes=[
                vmem(*diag.shape),
                vmem(*lower.shape),
                vmem(*vinv.shape),
                vmem(*upper.shape),
                vmem(levels - 1, pair, width),
                vmem(2, pair, width),
                vmem(3, slots, width // NX, width),
                [
                    vmem(CHIPS_Z[l], NC, slots, NX, width // NX, width)
                    for l in range(3)
                ],
                [vmem(SIZES[l], *tile) for l in range(3)],
                pltpu.SMEM((1, 128), jnp.int32),
                pltpu.SMEM((16, 128), jnp.int32),
                vmem(levels, slots, part, width),
                vmem(*split),
                vmem(*split),
                vmem(NX, levels, slots, part, width),
                vmem(levels - 1, *tile, dtype=F32),
                vmem(levels, *tile),
                vmem(4, pair, width),
                vmem(sum(SIZES[1:4]) + 32, *tile),
                vmem(NX, 4, *tile),
                vmem(16, *tile),
                [vmem(n, *tile) for n in (8, 16, 32, 32)],
                vmem(2, *tile),
                vmem(32, NC, *tile),
                vmem(32, *tile),
                dma((8,)),
                dma((11,)),
                dma((11,)),
                dma((NX - 1,)),
                dma((NX - 1,)),
                dma((3, 3)),
                dma((3, 3)),
                dma((3,)),
                dma((3,)),
                dma((levels,)),
            ],
            compiler_params=pltpu.CompilerParams(
                collective_id=0, has_side_effects=True
            ),
        )(
            parent.T,
            live_count.T,
            rhs.reshape(levels, slots, NX, part, width),
            upd.reshape(levels, slots, NX, part, width),
            diag,
            lower,
            vinv,
            upper,
        )
        result = result.reshape(levels, NX, slots, part, width)
        return result.transpose(0, 2, 1, 3, 4).reshape(rhs.shape)

    return jax.shard_map(
        on_device,
        mesh=mesh,
        in_specs=(
            P(None, "grid", None, None),
            P("gz", None, "grid", None, None),
            P(None, "grid", None, None),
            P(None, "grid", None, None),
            P(None, "grid", None, None),
            P(None, "grid", None, None),
            P(None, "grid"),
            P(None, "grid"),
        ),
        out_specs=P(None, "grid", None, None),
        check_vma=False,
    )
```

```python
import functools

import jax
import jax.numpy as jnp
from jax import lax
from jax.experimental import pallas as pl
from jax.experimental.pallas import tpu as pltpu
from jax.sharding import PartitionSpec as P

MESH = pl.DeviceIdType.MESH
F32 = jnp.float32
BF16 = jnp.bfloat16
NX, NY, NZ, NC = 4, 4, 8, 2
LEVELS = 6
CHIPS_Z = (2, 4, 8, 8, 8)
CHIPS_Y = (1, 1, 1, 2, 4)
SIZES = tuple(NC * a * b for a, b in zip(CHIPS_Z, CHIPS_Y))


def ring(k, n):
    return min(k, n - k)


def offsets(mz, my, cores):
    every = [
        (dy, dz, dc) for dy in range(my) for dz in range(mz) for dc in range(cores)
    ]
    every.sort(key=lambda o: -(ring(o[0], NY) + ring(o[1], NZ)))
    return [o for o in every if o != (0, 0, 0)]


def kernel(
    parent,
    live_count,
    rhs,
    upd,
    diag_hbm,
    lower_hbm,
    vinv_hbm,
    upper_hbm,
    out,
    diag,
    lower,
    vinv,
    upper,
    ml,
    uv_own,
    uv_part,
    tabs,
    picks,
    ftabs,
    ids_own,
    ids,
    rhs_own,
    rhs_first,
    upd_first,
    upd_all,
    fv,
    sol,
    chain,
    build,
    build0,
    in0,
    ins,
    mate,
    top_tab,
    load_sem,
    send,
    recv,
    rs_send,
    rs_recv,
    tab_send,
    tab_recv,
    ring_send,
    ring_recv,
    pick_send,
    pick_recv,
    f_send,
    f_recv,
    own_sem,
):
    x = lax.axis_index("gz")
    g = lax.axis_index("grid")
    y, z, c = g // (NZ * NC), lax.rem(g // NC, NZ), lax.rem(g, NC)

    zs = {m: [z // m * m + lax.rem(z + k, m) for k in range(m)] for m in (2, 4, 8)}
    ys = {m: [y // m * m + lax.rem(y + k, m) for k in range(m)] for m in (1, 2, 4)}
    cs = [c, 1 - c]
    xs = [lax.rem(x + k, NX) for k in range(NX)]

    def at(off, mz, my):
        dy, dz, dc = off
        return (ys[my][dy] * NZ + zs[mz][dz]) * NC + cs[dc]

    def remote(src, dst, s, r, gx, gg):
        return pltpu.make_async_remote_copy(
            src_ref=src,
            dst_ref=dst,
            send_sem=s,
            recv_sem=r,
            device_id=(gx, gg),
            device_id_type=MESH,
        )

    def wait(view, sem):
        pltpu.make_async_copy(view, view, sem).wait()

    barrier = pltpu.get_barrier_semaphore()
    near = [(k, g) for k in xs[1:]]
    near += [(k, at(o, 2, 1)) for k in xs for o in offsets(2, 1, 2)]
    near += [(x, at((dy, 0, 0), 8, 4)) for dy in (1, 3)]
    far = [(0, dz, dc) for dz in (1, 2, 6, 7) for dc in (0, 1)]
    for gx, gg in near:
        pl.semaphore_signal(barrier, inc=1, device_id=(gx, gg), device_id_type=MESH)
    for o in far:
        pl.semaphore_signal(
            barrier, inc=1, device_id=(x, at(o, 8, 4)), device_id_type=MESH
        )

    loads = [
        pltpu.make_async_copy(upd.at[0], upd_first, load_sem.at[0]),
        pltpu.make_async_copy(rhs.at[0], rhs_first, load_sem.at[1]),
        pltpu.make_async_copy(diag_hbm, diag, load_sem.at[2]),
        pltpu.make_async_copy(lower_hbm, lower, load_sem.at[3]),
        pltpu.make_async_copy(vinv_hbm, vinv, load_sem.at[4]),
        pltpu.make_async_copy(upper_hbm, upper, load_sem.at[5]),
        pltpu.make_async_copy(rhs.at[:, :, x], rhs_own, load_sem.at[6]),
        pltpu.make_async_copy(upd.at[:, :, x], upd_all.at[0], load_sem.at[7]),
    ]
    for copy in loads:
        copy.start()
    for l in range(LEVELS - 1):
        for s in range(2):
            ids_own[0, 2 * l + s] = parent[s, l]

    row = lax.broadcasted_iota(jnp.int32, (16, 128), 0)
    slotrow = row // 8

    def spread(v, half):
        rows = lax.broadcasted_iota(jnp.int32, v.shape, 0)
        zero = jnp.zeros_like(v)
        return jnp.concatenate(
            [jnp.where(rows < half, v, zero), jnp.where(rows < half, zero, v)], axis=1
        ).astype(BF16)

    def live_of(l, rows=16):
        slot = lax.broadcasted_iota(jnp.int32, (rows, 128), 0) // (rows // 2)
        return (slot < live_count[0, l]).astype(F32)

    def dot(a, b):
        return jnp.dot(a, b, preferred_element_type=F32)

    def mats(ref, l):
        return ref[l].reshape(256, 128)

    def twice(v):
        return jnp.concatenate([v, v], axis=0)

    def target(p, n):
        return lax.rem(p, 2 * n) - slotrow

    def product(a, b, dst, l):
        for s in range(2):
            dst[l, pl.ds(128 * s, 128), :] = dot(a[l, s], b[l, s]).astype(BF16)

    for k in range(4):
        loads[k].wait()
    first = rhs_first[...].astype(F32).reshape(64, 128) * (x == 0).astype(F32)
    first = first - upd_first[...].astype(F32).reshape(64, 128)
    f0 = dot(spread(first, 32), mats(diag, 0)) * live_of(0, 64)
    sent = dot(spread(f0, 32), mats(lower, 0))
    off0 = [(0, 0, 0)] + offsets(2, 1, 2)
    rels = [lax.rem(at(o, 2, 1), 4) for o in off0]
    pa, pb = target(parent[0, 0], 4), target(parent[1, 0], 4)
    for q in range(NX):
        a = twice(sent[8 * q : 8 * q + 8])
        b = twice(sent[32 + 8 * q : 40 + 8 * q])
        zero = jnp.zeros_like(a)
        for k, rel in enumerate(rels):
            build0[q, k] = (
                jnp.where(pa == 2 * rel, a, zero) + jnp.where(pb == 2 * rel, b, zero)
            ).astype(BF16)

    pl.semaphore_wait(barrier, len(near) + len(far))

    for dx in (2, 1, 3, 0):
        for k, o in enumerate(off0):
            if dx or k:
                remote(
                    build0.at[xs[dx], k],
                    in0.at[4 * dx + k],
                    send.at[0],
                    recv.at[0],
                    xs[dx],
                    at(o, 2, 1),
                ).start()
    rs = [
        remote(
            upd.at[:, :, xs[k]],
            upd_all.at[k],
            rs_send.at[k - 1],
            rs_recv.at[k - 1],
            xs[k],
            g,
        )
        for k in range(1, NX)
    ]
    for copy in rs:
        copy.start()

    for k in range(4, 8):
        loads[k].wait()
    partner = at((0, 0, 1), 2, 1)
    part = pl.ds(32 * x, 32)
    up_row = lax.rem(y, 2)
    homes = [lax.rem(z, 2), lax.rem(z, 4), z, up_row * NZ + z]

    for l in (1, 2, 3, 4):
        for s in range(2):
            live = (s < live_count[0, l]).astype(F32)
            quarter = (dot(upper[l, s, part, :], vinv[l, s]) * live).astype(BF16)
            uv_part[l - 1, s] = quarter
            tabs[l - 1][homes[l - 1], c, s] = quarter

    def table_direct(l):
        nz = CHIPS_Z[l - 1]
        for o in offsets(nz, 1, 1):
            remote(
                uv_part.at[l - 1],
                tabs[l - 1].at[homes[l - 1], c],
                tab_send.at[0, l - 1],
                tab_recv.at[0, l - 1],
                x,
                at(o, nz, 1),
            ).start()

    def direct_view(l):
        return tabs[l - 1].at[pl.ds(0, CHIPS_Z[l - 1] - 1), 0]

    def table_ring(step):
        for i, first in ((0, 0), (1, up_row * NZ)):
            tab = tabs[2 + i]
            if step == 3:
                moves = [(z, (0, 4, 0))]
            else:
                moves = [
                    (lax.rem(z + NZ - step, NZ), (0, 1, 0)),
                    (lax.rem(z + step, NZ), (0, 7, 0)),
                ]
            for block, o in moves:
                remote(
                    tab.at[first + block, c] if step else uv_part.at[2 + i],
                    tab.at[first + block, c],
                    ring_send.at[i, step],
                    ring_recv.at[i, step],
                    x,
                    at(o, 8, 1),
                ).start()

    def ring_view(i, step):
        return tabs[2 + i].at[pl.ds(0, 1 if step == 3 else 2), 0]

    def ring_wait(step):
        for i in range(2):
            wait(ring_view(i, step), ring_recv.at[i, step])

    rows_view = tabs[3].at[pl.ds(up_row * NZ, NZ), c]

    def rows_swap():
        remote(
            rows_view,
            rows_view,
            tab_send.at[0, 3],
            tab_recv.at[0, 3],
            x,
            at((1, 0, 0), 8, 2),
        ).start()

    def core_swap(l):
        tab = tabs[l - 1]
        remote(
            tab.at[:, c],
            tab.at[:, c],
            tab_send.at[1, l - 1],
            tab_recv.at[1, l - 1],
            x,
            partner,
        ).start()

    def core_view(l):
        return tabs[l - 1].at[:, 0]

    def pick_share(i):
        for k in (2, 1, 3):
            remote(
                picks[i].at[:, x],
                picks[i].at[:, x],
                pick_send.at[i],
                pick_recv.at[i],
                xs[k],
                g,
            ).start()

    def pick_view(i):
        return picks[i].at[:, pl.ds(0, NX - 1)]

    def f_share(l):
        n, nz, ny = SIZES[l - 1], CHIPS_Z[l - 1], CHIPS_Y[l - 1]
        mine = lax.rem(g, n)
        tile = fv[l].astype(BF16)
        ftabs[l - 1][mine] = tile
        for o in offsets(nz, ny, 2):
            remote(
                ftabs[l - 1].at[mine],
                ftabs[l - 1].at[mine],
                f_send.at[l - 1],
                f_recv.at[l - 1],
                x,
                at(o, nz, ny),
            ).start()

    def forward(l, total):
        fwd = dot(spread(total, 8), mats(diag, l)) * live_of(l)
        fv[l] = dot(spread(fwd, 8), mats(vinv, l)) * live_of(l)

    def base(l):
        total = rhs_own[l].astype(F32).reshape(16, 128)
        for k in range(NX):
            total = total - upd_all[k, l].astype(F32).reshape(16, 128)
        return total

    table_direct(1)
    table_ring(0)
    product(diag, lower, ml, 1)
    for copy in rs:
        copy.wait_recv()
    bases = base(1)
    wait(in0.at[pl.ds(1, 15)], recv.at[0])
    incoming = build0[x, 0].astype(F32)
    for k in range(1, 16):
        incoming = incoming + in0[k].astype(F32)

    for l in (1, 2, 3):
        n, mz, my = SIZES[l], CHIPS_Z[l], CHIPS_Y[l]
        total = bases - incoming
        sent = dot(spread(total, 8), ml[l]) * live_of(l)
        a, b = twice(sent[:8]), twice(sent[8:])
        zero = jnp.zeros_like(a)
        pa, pb = target(parent[0, l], n), target(parent[1, l], n)

        def tile(rel):
            return (
                jnp.where(pa == 2 * rel, a, zero) + jnp.where(pb == 2 * rel, b, zero)
            ).astype(BF16)

        offs = offsets(mz, my, 2)
        goals = [at(o, mz, my) for o in offs]
        start = sum(SIZES[1:l])
        for k, goal in enumerate(goals):
            build[start + k] = tile(lax.rem(goal, n))
        for k, goal in enumerate(goals):
            remote(
                build.at[start + k], ins[l - 1].at[k], send.at[l], recv.at[l], x, goal
            ).start()
        own = tile(lax.rem(g, n)).astype(F32)

        forward(l, total)
        f_share(l)
        if l == 1:
            table_direct(2)
            ring_wait(0)
            table_ring(1)
            forward(0, base(0))
        if l == 2:
            mine = lax.rem(g, 32)
            for s in range(10):
                ids[mine, s] = ids_own[0, s]
            for o in offsets(8, 1, 2):
                remote(
                    ids_own,
                    ids.at[pl.ds(mine, 1)],
                    send.at[8],
                    recv.at[8],
                    x,
                    at(o, 8, 1),
                ).start()
            ring_wait(1)
            table_ring(2)
            table_ring(3)
            for j in (1, 2):
                wait(direct_view(j), tab_recv.at[0, j - 1])
                core_swap(j)
        if l == 3:
            ring_wait(2)
            ring_wait(3)
            rows_swap()
            core_swap(3)
            wait(ids.at[pl.ds(0, 15)], recv.at[8])
            half_ids = ids.at[pl.ds(16 * up_row, 16)]
            remote(
                half_ids, half_ids, send.at[7], recv.at[7], x, at((1, 0, 0), 8, 2)
            ).start()
        product(diag, lower, ml, l + 1)
        product(upper, vinv, uv_own, l)
        if l == 3:
            for j in (1, 2, 3):
                wait(core_view(j), tab_recv.at[1, j - 1])
            wait(half_ids, recv.at[7])
            chains = []
            for k in range(4):
                for s in range(2):
                    path = {}
                    p = parent[s, k]
                    for j in range(k + 1, 5):
                        n = SIZES[j - 1]
                        path[j] = lax.rem(p, 2 * n)
                        p = ids[
                            lax.rem(path[j] // 2, n) + (g // n * n - g // 32 * 32),
                            2 * j + lax.rem(path[j], 2),
                        ]
                    path[5] = lax.rem(p, 128)
                    chains.append(path)
            places = {}
            for k in range(3):
                for s in range(2):
                    for j in range(k + 1, 4):
                        p = chains[2 * k + s][j]
                        places[k, s, j] = len(places)
                        picks[0][places[k, s, j], x] = tabs[j - 1][
                            p // 4, lax.rem(p // 2, 2), lax.rem(p, 2)
                        ]
            pick_share(0)
            wait(rows_view, tab_recv.at[0, 3])
            core_swap(4)
        bases = base(l + 1)
        wait(ins[l - 1].at[pl.ds(0, n - 1)], recv.at[l])
        incoming = own
        for k in range(n - 1):
            incoming = incoming + ins[l - 1][k].astype(F32)

    total = bases - incoming
    sent = dot(spread(total, 8), ml[4]) * live_of(4)
    mate[0] = sent.astype(BF16)
    remote(mate.at[0], mate.at[1], send.at[5], recv.at[5], x, partner).start()
    pa, pb = target(parent[0, 4], 64), target(parent[1, 4], 64)
    other = lax.rem(partner, 32)
    pc, pd = target(ids[other, 8], 64), target(ids[other, 9], 64)
    offs = offsets(8, 4, 1)
    goals = [at(o, 8, 4) for o in offs]
    a, b = twice(sent[:8]), twice(sent[8:])
    bases = base(5)
    wait(mate.at[1], recv.at[5])
    third = mate[1].astype(F32)
    d, e = twice(third[:8]), twice(third[8:])
    zero = jnp.zeros_like(a)

    def tile4(goal):
        return (
            jnp.where(pa == 2 * goal, a, zero)
            + jnp.where(pb == 2 * goal, b, zero)
            + jnp.where(pc == 2 * goal, d, zero)
            + jnp.where(pd == 2 * goal, e, zero)
        ).astype(BF16)

    start = sum(SIZES[1:4])
    for k, goal in enumerate(goals):
        build[start + k] = tile4(goal)
    for k, goal in enumerate(goals):
        remote(
            build.at[start + k], ins[3].at[k], send.at[4], recv.at[4], x, goal
        ).start()
    own = tile4(g).astype(F32)
    wait(core_view(4), tab_recv.at[1, 3])
    for k in range(4):
        for s in range(2):
            p = chains[2 * k + s][4]
            picks[1][2 * k + s, x] = tabs[3][p // 4, lax.rem(p // 2, 2), lax.rem(p, 2)]
    pick_share(1)
    forward(4, total)
    f_share(4)
    product(upper, vinv, uv_own, 4)
    product(upper, vinv, uv_own, 0)

    wait(pick_view(0), pick_recv.at[0])
    for j in (1, 2, 3):
        wait(ftabs[j - 1].at[pl.ds(0, SIZES[j - 1] - 1)], f_recv.at[j - 1])

    def half(t, p):
        t = t.astype(F32)
        return jnp.where(lax.rem(p, 2) == 0, t[:8], t[8:])

    for k in range(4):
        consts = []
        for s in range(2):
            path = chains[2 * k + s]
            m = const = None
            for j in range(3, k - 1, -1):
                if j == k:
                    u = uv_own[k, pl.ds(128 * s, 128), :]
                    f = fv[k, pl.ds(8 * s, 8), :]
                else:
                    u = picks[0][places[k, s, j]].reshape(128, 128)
                    f = half(ftabs[j - 1][path[j] // 2], path[j])
                if m is None:
                    m, const = u, f
                else:
                    const = f - dot(const.astype(BF16), u)
                    m = dot(m, u).astype(BF16)
            chain[k, pl.ds(128 * s, 128), :] = m
            consts.append(const)
        fv[k] = jnp.concatenate(consts, axis=0)
    wait(ins[3].at[pl.ds(0, 31)], recv.at[4])
    incoming = own
    for k in range(31):
        incoming = incoming + ins[3][k].astype(F32)

    fwd = dot(spread(bases - incoming, 8), mats(diag, 5)) * live_of(5)
    sol[5] = (dot(spread(fwd, 8), mats(vinv, 5)) * live_of(5)).astype(BF16)

    def share(first, count):
        span = pl.ds(first, count)
        for k in (2, 1, 3):
            remote(
                sol.at[span], out.at[span, x], send.at[9], recv.at[9], xs[k], g
            ).start()
        pltpu.make_async_copy(
            sol.at[span], out.at[span, x], own_sem.at[first]
        ).start()

    chip = y * NZ + z
    for o in offs:
        remote(
            sol.at[5], top_tab.at[chip, c], send.at[6], recv.at[6], x, at(o, 8, 4)
        ).start()
    top_tab[chip, c] = sol[5]
    share(5, 1)

    wait(pick_view(1), pick_recv.at[1])
    wait(ftabs[3].at[pl.ds(0, 31)], f_recv.at[3])
    for k in range(4):
        sign = 1 if k % 2 == 0 else -1
        ends = [chains[2 * k + s][4] for s in range(2)]
        f = jnp.concatenate([half(ftabs[3][p // 2], p) for p in ends], axis=0)
        fv[k] = fv[k] + sign * dot(spread(f, 8), chain[k])
        for s in range(2):
            span = pl.ds(128 * s, 128)
            u = picks[1][2 * k + s].reshape(128, 128)
            chain[k, span, :] = dot(u, chain[k, span, :]).astype(BF16)
    for s in range(2):
        chain[4, pl.ds(128 * s, 128), :] = uv_own[4, pl.ds(128 * s, 128), :]

    wait(top_tab.at[pl.ds(0, 31), 0], recv.at[6])
    remote(
        top_tab.at[:, c], top_tab.at[:, c], send.at[10], recv.at[10], x, partner
    ).start()
    wait(top_tab.at[:, 0], recv.at[10])
    for k in range(5):
        if k < 4:
            ends = [chains[2 * k + s][5] for s in range(2)]
        else:
            ends = [lax.rem(parent[s, 4], 128) for s in range(2)]
        above = jnp.concatenate(
            [half(top_tab[p // 4, lax.rem(p // 2, 2)], p) for p in ends], axis=0
        )
        low = dot(spread(above, 8), chain[k])
        value = fv[k] + low if k % 2 == 1 else fv[k] - low
        sol[k] = (value * live_of(k)).astype(BF16)
    share(0, 5)

    wait(in0.at[pl.ds(1, 15)], send.at[0])
    for copy in rs:
        copy.wait_send()
    for l in (1, 2, 3):
        wait(ins[l - 1].at[pl.ds(0, SIZES[l] - 1)], send.at[l])
        if l < 3:
            wait(direct_view(l), tab_send.at[0, l - 1])
    for step in range(4):
        for i in range(2):
            wait(ring_view(i, step), ring_send.at[i, step])
    wait(rows_view, tab_send.at[0, 3])
    for l in (1, 2, 3, 4):
        wait(core_view(l), tab_send.at[1, l - 1])
        wait(ftabs[l - 1].at[pl.ds(0, SIZES[l - 1] - 1)], f_send.at[l - 1])
    for i in range(2):
        wait(pick_view(i), pick_send.at[i])
    wait(ins[3].at[pl.ds(0, 31)], send.at[4])
    wait(mate.at[0], send.at[5])
    wait(top_tab.at[pl.ds(0, 31), 0], send.at[6])
    wait(half_ids, send.at[7])
    wait(ids.at[pl.ds(0, 15)], send.at[8])
    wait(top_tab.at[:, 0], send.at[10])
    for first, count in ((5, 1), (0, 5)):
        span = pl.ds(first, count)
        pltpu.make_async_copy(
            sol.at[span], out.at[span, x], own_sem.at[first]
        ).wait()
    whole = out.at[:, pl.ds(0, NX - 1)]
    wait(whole, send.at[9])
    wait(whole, recv.at[9])


def solution(mesh):
    def on_device(rhs, upd, diag, lower, vinv, upper, parent, live_count):
        levels, slots, rows, width = rhs.shape
        part = rows // NX
        hbm = pl.BlockSpec(memory_space=pl.ANY)
        smem = pl.BlockSpec(memory_space=pltpu.SMEM)
        dma = pltpu.SemaphoreType.DMA
        pair = slots * width
        tile = (slots * part, width)
        split = (slots, NX, part, width)

        def vmem(*shape, dtype=BF16):
            return pltpu.VMEM(shape, dtype)

        result = pl.pallas_call(
            kernel,
            out_shape=jax.ShapeDtypeStruct((levels, NX) + tile, BF16),
            in_specs=[smem, smem] + [hbm] * 6,
            out_specs=hbm,
            scratch_shapes=[
                vmem(*diag.shape),
                vmem(*lower.shape),
                vmem(*vinv.shape),
                vmem(*upper.shape),
                vmem(levels - 1, pair, width),
                vmem(levels - 1, pair, width),
                vmem(4, slots, width // NX, width),
                [vmem(SIZES[l] // NC, NC, slots, width // NX, width) for l in range(4)],
                [vmem(n, NX, width // NX, width) for n in (12, 8)],
                [vmem(SIZES[l], *tile) for l in range(4)],
                pltpu.SMEM((1, 128), jnp.int32),
                pltpu.SMEM((32, 128), jnp.int32),
                vmem(levels, slots, part, width),
                vmem(*split),
                vmem(*split),
                vmem(NX, levels, slots, part, width),
                vmem(levels - 1, *tile, dtype=F32),
                vmem(levels, *tile),
                vmem(levels - 1, pair, width),
                vmem(sum(SIZES[1:4]) + 32, *tile),
                vmem(NX, 4, *tile),
                vmem(16, *tile),
                [vmem(n, *tile) for n in (8, 16, 32, 32)],
                vmem(2, *tile),
                vmem(32, NC, *tile),
                dma((8,)),
                dma((11,)),
                dma((11,)),
                dma((NX - 1,)),
                dma((NX - 1,)),
                dma((2, 4)),
                dma((2, 4)),
                dma((2, 4)),
                dma((2, 4)),
                dma((2,)),
                dma((2,)),
                dma((4,)),
                dma((4,)),
                dma((levels,)),
            ],
            compiler_params=pltpu.CompilerParams(
                collective_id=0, has_side_effects=True
            ),
        )(
            parent.T,
            live_count.T,
            rhs.reshape(levels, slots, NX, part, width),
            upd.reshape(levels, slots, NX, part, width),
            diag,
            lower,
            vinv,
            upper,
        )
        result = result.reshape(levels, NX, slots, part, width)
        return result.transpose(0, 2, 1, 3, 4).reshape(rhs.shape)

    return jax.shard_map(
        on_device,
        mesh=mesh,
        in_specs=(
            P(None, "grid", None, None),
            P("gz", None, "grid", None, None),
            P(None, "grid", None, None),
            P(None, "grid", None, None),
            P(None, "grid", None, None),
            P(None, "grid", None, None),
            P(None, "grid"),
            P(None, "grid"),
        ),
        out_specs=P(None, "grid", None, None),
        check_vma=False,
    )
```

```python
import functools

import jax
import jax.numpy as jnp
from jax import lax
from jax.experimental import pallas as pl
from jax.experimental.pallas import tpu as pltpu
from jax.sharding import PartitionSpec as P

MESH = pl.DeviceIdType.MESH
F32 = jnp.float32
BF16 = jnp.bfloat16
NX, NY, NZ, NC = 4, 4, 8, 2
LEVELS = 6
CHIPS_Z = (2, 4, 8, 8, 8)
CHIPS_Y = (1, 1, 1, 2, 4)
SIZES = tuple(NC * a * b for a, b in zip(CHIPS_Z, CHIPS_Y))


def ring(k, n):
    return min(k, n - k)


def offsets(mz, my, cores):
    every = [
        (dy, dz, dc) for dy in range(my) for dz in range(mz) for dc in range(cores)
    ]
    every.sort(key=lambda o: -(ring(o[0], NY) + ring(o[1], NZ)))
    return [o for o in every if o != (0, 0, 0)]


def kernel(
    parent,
    live_count,
    rhs,
    upd,
    diag_hbm,
    lower_hbm,
    vinv_hbm,
    upper_hbm,
    out,
    diag,
    lower,
    vinv,
    upper,
    ml,
    uv_own,
    uv_part,
    tabs,
    picks,
    ftabs,
    ids_own,
    ids,
    rhs_own,
    rhs_first,
    upd_first,
    upd_all,
    fv,
    sol,
    chain,
    build,
    build0,
    in0,
    ins,
    mate,
    top_tab,
    load_sem,
    send,
    recv,
    rs_send,
    rs_recv,
    tab_send,
    tab_recv,
    ring_send,
    ring_recv,
    swap_send,
    swap_recv,
    pick_send,
    pick_recv,
    f_send,
    f_recv,
    own_sem,
):
    x = lax.axis_index("gz")
    g = lax.axis_index("grid")
    y, z, c = g // (NZ * NC), lax.rem(g // NC, NZ), lax.rem(g, NC)

    zs = {m: [z // m * m + lax.rem(z + k, m) for k in range(m)] for m in (2, 4, 8)}
    ys = {m: [y // m * m + lax.rem(y + k, m) for k in range(m)] for m in (1, 2, 4)}
    cs = [c, 1 - c]
    xs = [lax.rem(x + k, NX) for k in range(NX)]

    def at(off, mz, my):
        dy, dz, dc = off
        return (ys[my][dy] * NZ + zs[mz][dz]) * NC + cs[dc]

    def remote(src, dst, s, r, gx, gg):
        return pltpu.make_async_remote_copy(
            src_ref=src,
            dst_ref=dst,
            send_sem=s,
            recv_sem=r,
            device_id=(gx, gg),
            device_id_type=MESH,
        )

    def wait(view, sem):
        pltpu.make_async_copy(view, view, sem).wait()

    barrier = pltpu.get_barrier_semaphore()
    near = [(k, g) for k in xs[1:]]
    near += [(k, at(o, 2, 1)) for k in xs for o in offsets(2, 1, 2)]
    near += [(x, at((dy, 0, 0), 8, 4)) for dy in (1, 3)]
    far = [(0, dz, dc) for dz in (1, 2, 6, 7) for dc in (0, 1)]
    for gx, gg in near:
        pl.semaphore_signal(barrier, inc=1, device_id=(gx, gg), device_id_type=MESH)
    for o in far:
        pl.semaphore_signal(
            barrier, inc=1, device_id=(x, at(o, 8, 4)), device_id_type=MESH
        )

    loads = [
        pltpu.make_async_copy(upd.at[0], upd_first, load_sem.at[0]),
        pltpu.make_async_copy(rhs.at[0], rhs_first, load_sem.at[1]),
        pltpu.make_async_copy(diag_hbm, diag, load_sem.at[2]),
        pltpu.make_async_copy(lower_hbm, lower, load_sem.at[3]),
        pltpu.make_async_copy(vinv_hbm, vinv, load_sem.at[4]),
        pltpu.make_async_copy(upper_hbm, upper, load_sem.at[5]),
        pltpu.make_async_copy(rhs.at[:, :, x], rhs_own, load_sem.at[6]),
        pltpu.make_async_copy(upd.at[:, :, x], upd_all.at[0], load_sem.at[7]),
    ]
    for copy in loads:
        copy.start()
    for l in range(LEVELS - 1):
        for s in range(2):
            ids_own[0, 2 * l + s] = parent[s, l]

    row = lax.broadcasted_iota(jnp.int32, (16, 128), 0)
    slotrow = row // 8

    def spread(v, half):
        rows = lax.broadcasted_iota(jnp.int32, v.shape, 0)
        zero = jnp.zeros_like(v)
        return jnp.concatenate(
            [jnp.where(rows < half, v, zero), jnp.where(rows < half, zero, v)], axis=1
        ).astype(BF16)

    def live_of(l, rows=16):
        slot = lax.broadcasted_iota(jnp.int32, (rows, 128), 0) // (rows // 2)
        return (slot < live_count[0, l]).astype(F32)

    def dot(a, b):
        return jnp.dot(a, b, preferred_element_type=F32)

    def mats(ref, l):
        return ref[l].reshape(256, 128)

    def twice(v):
        return jnp.concatenate([v, v], axis=0)

    def target(p, n):
        return lax.rem(p, 2 * n) - slotrow

    def product(a, b, dst, l):
        for s in range(2):
            dst[l, pl.ds(128 * s, 128), :] = dot(a[l, s], b[l, s]).astype(BF16)

    for k in range(4):
        loads[k].wait()
    first = rhs_first[...].astype(F32).reshape(64, 128) * (x == 0).astype(F32)
    first = first - upd_first[...].astype(F32).reshape(64, 128)
    f0 = dot(spread(first, 32), mats(diag, 0)) * live_of(0, 64)
    sent = dot(spread(f0, 32), mats(lower, 0))
    off0 = [(0, 0, 0)] + offsets(2, 1, 2)
    rels = [lax.rem(at(o, 2, 1), 4) for o in off0]
    pa, pb = target(parent[0, 0], 4), target(parent[1, 0], 4)
    for q in range(NX):
        a = twice(sent[8 * q : 8 * q + 8])
        b = twice(sent[32 + 8 * q : 40 + 8 * q])
        zero = jnp.zeros_like(a)
        for k, rel in enumerate(rels):
            build0[q, k] = (
                jnp.where(pa == 2 * rel, a, zero) + jnp.where(pb == 2 * rel, b, zero)
            ).astype(BF16)

    pl.semaphore_wait(barrier, len(near) + len(far))

    for dx in (2, 1, 3, 0):
        for k, o in enumerate(off0):
            if dx or k:
                remote(
                    build0.at[xs[dx], k],
                    in0.at[4 * dx + k],
                    send.at[0],
                    recv.at[0],
                    xs[dx],
                    at(o, 2, 1),
                ).start()
    rs = [
        remote(
            upd.at[:, :, xs[k]],
            upd_all.at[k],
            rs_send.at[k - 1],
            rs_recv.at[k - 1],
            xs[k],
            g,
        )
        for k in range(1, NX)
    ]
    for copy in rs:
        copy.start()

    for k in range(4, 8):
        loads[k].wait()
    partner = at((0, 0, 1), 2, 1)
    part = pl.ds(32 * x, 32)
    up_row = lax.rem(y, 2)
    homes = [lax.rem(z, 2), lax.rem(z, 4), z, up_row * NZ + z]

    for l in (1, 2, 3, 4):
        for s in range(2):
            live = (s < live_count[0, l]).astype(F32)
            quarter = (dot(upper[l, s, part, :], vinv[l, s]) * live).astype(BF16)
            uv_part[l - 1, s] = quarter
            tabs[l - 1][homes[l - 1], c, s] = quarter

    def table_direct(l):
        nz = CHIPS_Z[l - 1]
        for o in offsets(nz, 1, 1):
            remote(
                uv_part.at[l - 1],
                tabs[l - 1].at[homes[l - 1], c],
                tab_send.at[0, l - 1],
                tab_recv.at[0, l - 1],
                x,
                at(o, nz, 1),
            ).start()

    def direct_view(l):
        return tabs[l - 1].at[pl.ds(0, CHIPS_Z[l - 1] - 1), 0]

    def table_ring(step):
        for i, first in ((0, 0), (1, up_row * NZ)):
            tab = tabs[2 + i]
            if step == 3:
                moves = [(z, (0, 4, 0))]
            else:
                moves = [
                    (lax.rem(z + NZ - step, NZ), (0, 1, 0)),
                    (lax.rem(z + step, NZ), (0, 7, 0)),
                ]
            for block, o in moves:
                remote(
                    tab.at[first + block, c] if step else uv_part.at[2 + i],
                    tab.at[first + block, c],
                    ring_send.at[i, step],
                    ring_recv.at[i, step],
                    x,
                    at(o, 8, 1),
                ).start()

    def ring_view(i, step):
        return tabs[2 + i].at[pl.ds(0, 1 if step == 3 else 2), 0]

    def ring_wait(step):
        for i in range(2):
            wait(ring_view(i, step), ring_recv.at[i, step])

    swaps = ((0, 1, 7), (2, 6), (3, 5, 4))

    def rows_swap(step):
        for k in swaps[step]:
            block = tabs[3].at[up_row * NZ + zs[8][k], c]
            remote(
                block,
                block,
                swap_send.at[step],
                swap_recv.at[step],
                x,
                at((1, 0, 0), 8, 2),
            ).start()

    def rows_view(step):
        return tabs[3].at[pl.ds(0, len(swaps[step])), 0]

    def core_swap(l):
        tab = tabs[l - 1]
        remote(
            tab.at[:, c],
            tab.at[:, c],
            tab_send.at[1, l - 1],
            tab_recv.at[1, l - 1],
            x,
            partner,
        ).start()

    def core_view(l):
        return tabs[l - 1].at[:, 0]

    def pick_share(i):
        for k in (2, 1, 3):
            remote(
                picks[i].at[:, x],
                picks[i].at[:, x],
                pick_send.at[i],
                pick_recv.at[i],
                xs[k],
                g,
            ).start()

    def pick_view(i):
        return picks[i].at[:, pl.ds(0, NX - 1)]

    def f_share(l):
        nz, ny = CHIPS_Z[l - 1], CHIPS_Y[l - 1]
        tab = ftabs[l - 1]
        tab[homes[l - 1], c] = fv[l].astype(BF16)
        for o in offsets(nz, ny, 1):
            remote(
                tab.at[homes[l - 1], c],
                tab.at[homes[l - 1], c],
                f_send.at[0, l - 1],
                f_recv.at[0, l - 1],
                x,
                at(o, nz, ny),
            ).start()

    def f_view(l):
        return ftabs[l - 1].at[pl.ds(0, SIZES[l - 1] // NC - 1), 0]

    def f_swap(l):
        wait(f_view(l), f_recv.at[0, l - 1])
        tab = ftabs[l - 1]
        remote(
            tab.at[:, c],
            tab.at[:, c],
            f_send.at[1, l - 1],
            f_recv.at[1, l - 1],
            x,
            partner,
        ).start()

    def f_wait(l):
        wait(ftabs[l - 1].at[:, 0], f_recv.at[1, l - 1])

    def f_tile(l, p):
        return half(ftabs[l - 1][p // 4, lax.rem(p // 2, 2)], p)

    def half(t, p):
        t = t.astype(F32)
        return jnp.where(lax.rem(p, 2) == 0, t[:8], t[8:])

    def forward(l, total):
        fwd = dot(spread(total, 8), mats(diag, l)) * live_of(l)
        fv[l] = dot(spread(fwd, 8), mats(vinv, l)) * live_of(l)

    def base(l):
        total = rhs_own[l].astype(F32).reshape(16, 128)
        for k in range(NX):
            total = total - upd_all[k, l].astype(F32).reshape(16, 128)
        return total

    table_direct(1)
    table_ring(0)
    product(diag, lower, ml, 1)
    for copy in rs:
        copy.wait_recv()
    bases = base(1)
    wait(in0.at[pl.ds(1, 15)], recv.at[0])
    incoming = build0[x, 0].astype(F32)
    for k in range(1, 16):
        incoming = incoming + in0[k].astype(F32)

    for l in (1, 2, 3):
        n, mz, my = SIZES[l], CHIPS_Z[l], CHIPS_Y[l]
        total = bases - incoming
        sent = dot(spread(total, 8), ml[l]) * live_of(l)
        a, b = twice(sent[:8]), twice(sent[8:])
        zero = jnp.zeros_like(a)
        pa, pb = target(parent[0, l], n), target(parent[1, l], n)

        def tile(rel):
            return (
                jnp.where(pa == 2 * rel, a, zero) + jnp.where(pb == 2 * rel, b, zero)
            ).astype(BF16)

        offs = offsets(mz, my, 2)
        goals = [at(o, mz, my) for o in offs]
        start = sum(SIZES[1:l])
        for k, goal in enumerate(goals):
            build[start + k] = tile(lax.rem(goal, n))
        for k, goal in enumerate(goals):
            remote(
                build.at[start + k], ins[l - 1].at[k], send.at[l], recv.at[l], x, goal
            ).start()
        own = tile(lax.rem(g, n)).astype(F32)

        forward(l, total)
        f_share(l)
        if l == 1:
            table_direct(2)
            ring_wait(0)
            table_ring(1)
            rows_swap(0)
            forward(0, base(0))
        if l == 2:
            mine = lax.rem(g, 32)
            for s in range(10):
                ids[mine, s] = ids_own[0, s]
            for o in offsets(8, 1, 2):
                remote(
                    ids_own,
                    ids.at[pl.ds(mine, 1)],
                    send.at[8],
                    recv.at[8],
                    x,
                    at(o, 8, 1),
                ).start()
            ring_wait(1)
            table_ring(2)
            table_ring(3)
            rows_swap(1)
            for j in (1, 2):
                wait(direct_view(j), tab_recv.at[0, j - 1])
                core_swap(j)
        if l == 3:
            ring_wait(2)
            ring_wait(3)
            rows_swap(2)
            core_swap(3)
            wait(ids.at[pl.ds(0, 15)], recv.at[8])
            half_ids = ids.at[pl.ds(16 * up_row, 16)]
            remote(
                half_ids, half_ids, send.at[7], recv.at[7], x, at((1, 0, 0), 8, 2)
            ).start()
        product(diag, lower, ml, l + 1)
        product(upper, vinv, uv_own, l)
        if l == 3:
            for j in (1, 2, 3):
                wait(core_view(j), tab_recv.at[1, j - 1])
            wait(half_ids, recv.at[7])
            chains = []
            for k in range(4):
                for s in range(2):
                    path = {}
                    p = parent[s, k]
                    for j in range(k + 1, 5):
                        n = SIZES[j - 1]
                        path[j] = lax.rem(p, 2 * n)
                        p = ids[
                            lax.rem(path[j] // 2, n) + (g // n * n - g // 32 * 32),
                            2 * j + lax.rem(path[j], 2),
                        ]
                    path[5] = lax.rem(p, 128)
                    chains.append(path)
            places = {}
            for k in range(3):
                for s in range(2):
                    for j in range(k + 1, 4):
                        p = chains[2 * k + s][j]
                        places[k, s, j] = len(places)
                        picks[0][places[k, s, j], x] = tabs[j - 1][
                            p // 4, lax.rem(p // 2, 2), lax.rem(p, 2)
                        ]
            pick_share(0)
        bases = base(l + 1)
        wait(ins[l - 1].at[pl.ds(0, n - 1)], recv.at[l])
        incoming = own
        for k in range(n - 1):
            incoming = incoming + ins[l - 1][k].astype(F32)

    total = bases - incoming
    sent = dot(spread(total, 8), ml[4]) * live_of(4)
    mate[0] = sent.astype(BF16)
    remote(mate.at[0], mate.at[1], send.at[5], recv.at[5], x, partner).start()
    pa, pb = target(parent[0, 4], 64), target(parent[1, 4], 64)
    other = lax.rem(partner, 32)
    pc, pd = target(ids[other, 8], 64), target(ids[other, 9], 64)
    offs = offsets(8, 4, 1)
    goals = [at(o, 8, 4) for o in offs]
    a, b = twice(sent[:8]), twice(sent[8:])
    bases = base(5)
    wait(mate.at[1], recv.at[5])
    third = mate[1].astype(F32)
    d, e = twice(third[:8]), twice(third[8:])
    zero = jnp.zeros_like(a)

    def tile4(goal):
        return (
            jnp.where(pa == 2 * goal, a, zero)
            + jnp.where(pb == 2 * goal, b, zero)
            + jnp.where(pc == 2 * goal, d, zero)
            + jnp.where(pd == 2 * goal, e, zero)
        ).astype(BF16)

    start = sum(SIZES[1:4])
    for k, goal in enumerate(goals):
        build[start + k] = tile4(goal)
    for k, goal in enumerate(goals):
        remote(
            build.at[start + k], ins[3].at[k], send.at[4], recv.at[4], x, goal
        ).start()
    own = tile4(g).astype(F32)
    for j in (1, 2, 3):
        f_swap(j)
    for step in range(3):
        wait(rows_view(step), swap_recv.at[step])
    core_swap(4)
    forward(4, total)
    f_share(4)
    product(upper, vinv, uv_own, 4)
    product(upper, vinv, uv_own, 0)
    wait(core_view(4), tab_recv.at[1, 3])
    for k in range(4):
        for s in range(2):
            p = chains[2 * k + s][4]
            picks[1][2 * k + s, x] = tabs[3][p // 4, lax.rem(p // 2, 2), lax.rem(p, 2)]
    pick_share(1)

    wait(pick_view(0), pick_recv.at[0])
    for j in (1, 2, 3):
        f_wait(j)
    for k in range(4):
        consts = []
        for s in range(2):
            path = chains[2 * k + s]
            m = const = None
            for j in range(3, k - 1, -1):
                if j == k:
                    u = uv_own[k, pl.ds(128 * s, 128), :]
                    f = fv[k, pl.ds(8 * s, 8), :]
                else:
                    u = picks[0][places[k, s, j]].reshape(128, 128)
                    f = f_tile(j, path[j])
                if m is None:
                    m, const = u, f
                else:
                    const = f - dot(const.astype(BF16), u)
                    m = dot(m, u).astype(BF16)
            chain[k, pl.ds(128 * s, 128), :] = m
            consts.append(const)
        fv[k] = jnp.concatenate(consts, axis=0)
    wait(ins[3].at[pl.ds(0, 31)], recv.at[4])
    incoming = own
    for k in range(31):
        incoming = incoming + ins[3][k].astype(F32)

    fwd = dot(spread(bases - incoming, 8), mats(diag, 5)) * live_of(5)
    sol[5] = (dot(spread(fwd, 8), mats(vinv, 5)) * live_of(5)).astype(BF16)

    def share(first, count):
        span = pl.ds(first, count)
        for k in (2, 1, 3):
            remote(
                sol.at[span], out.at[span, x], send.at[9], recv.at[9], xs[k], g
            ).start()
        pltpu.make_async_copy(
            sol.at[span], out.at[span, x], own_sem.at[first]
        ).start()

    chip = y * NZ + z
    for o in offs:
        remote(
            sol.at[5], top_tab.at[chip, c], send.at[6], recv.at[6], x, at(o, 8, 4)
        ).start()
    top_tab[chip, c] = sol[5]
    share(5, 1)

    f_swap(4)
    wait(pick_view(1), pick_recv.at[1])
    f_wait(4)
    for k in range(4):
        sign = 1 if k % 2 == 0 else -1
        ends = [chains[2 * k + s][4] for s in range(2)]
        f = jnp.concatenate([f_tile(4, p) for p in ends], axis=0)
        fv[k] = fv[k] + sign * dot(spread(f, 8), chain[k])
        for s in range(2):
            span = pl.ds(128 * s, 128)
            u = picks[1][2 * k + s].reshape(128, 128)
            chain[k, span, :] = dot(u, chain[k, span, :]).astype(BF16)
    for s in range(2):
        chain[4, pl.ds(128 * s, 128), :] = uv_own[4, pl.ds(128 * s, 128), :]

    wait(top_tab.at[pl.ds(0, 31), 0], recv.at[6])
    remote(
        top_tab.at[:, c], top_tab.at[:, c], send.at[10], recv.at[10], x, partner
    ).start()
    wait(top_tab.at[:, 0], recv.at[10])
    for k in range(5):
        if k < 4:
            ends = [chains[2 * k + s][5] for s in range(2)]
        else:
            ends = [lax.rem(parent[s, 4], 128) for s in range(2)]
        above = jnp.concatenate(
            [half(top_tab[p // 4, lax.rem(p // 2, 2)], p) for p in ends], axis=0
        )
        low = dot(spread(above, 8), chain[k])
        value = fv[k] + low if k % 2 == 1 else fv[k] - low
        sol[k] = (value * live_of(k)).astype(BF16)
    share(0, 5)

    wait(in0.at[pl.ds(1, 15)], send.at[0])
    for copy in rs:
        copy.wait_send()
    for l in (1, 2, 3):
        wait(ins[l - 1].at[pl.ds(0, SIZES[l] - 1)], send.at[l])
        if l < 3:
            wait(direct_view(l), tab_send.at[0, l - 1])
    for step in range(4):
        for i in range(2):
            wait(ring_view(i, step), ring_send.at[i, step])
    for step in range(3):
        wait(rows_view(step), swap_send.at[step])
    for l in (1, 2, 3, 4):
        wait(core_view(l), tab_send.at[1, l - 1])
        wait(f_view(l), f_send.at[0, l - 1])
        wait(ftabs[l - 1].at[:, 0], f_send.at[1, l - 1])
    for i in range(2):
        wait(pick_view(i), pick_send.at[i])
    wait(ins[3].at[pl.ds(0, 31)], send.at[4])
    wait(mate.at[0], send.at[5])
    wait(top_tab.at[pl.ds(0, 31), 0], send.at[6])
    wait(half_ids, send.at[7])
    wait(ids.at[pl.ds(0, 15)], send.at[8])
    wait(top_tab.at[:, 0], send.at[10])
    for first, count in ((5, 1), (0, 5)):
        span = pl.ds(first, count)
        pltpu.make_async_copy(
            sol.at[span], out.at[span, x], own_sem.at[first]
        ).wait()
    whole = out.at[:, pl.ds(0, NX - 1)]
    wait(whole, send.at[9])
    wait(whole, recv.at[9])


def solution(mesh):
    def on_device(rhs, upd, diag, lower, vinv, upper, parent, live_count):
        levels, slots, rows, width = rhs.shape
        part = rows // NX
        hbm = pl.BlockSpec(memory_space=pl.ANY)
        smem = pl.BlockSpec(memory_space=pltpu.SMEM)
        dma = pltpu.SemaphoreType.DMA
        pair = slots * width
        tile = (slots * part, width)
        split = (slots, NX, part, width)

        def vmem(*shape, dtype=BF16):
            return pltpu.VMEM(shape, dtype)

        result = pl.pallas_call(
            kernel,
            out_shape=jax.ShapeDtypeStruct((levels, NX) + tile, BF16),
            in_specs=[smem, smem] + [hbm] * 6,
            out_specs=hbm,
            scratch_shapes=[
                vmem(*diag.shape),
                vmem(*lower.shape),
                vmem(*vinv.shape),
                vmem(*upper.shape),
                vmem(levels - 1, pair, width),
                vmem(levels - 1, pair, width),
                vmem(4, slots, width // NX, width),
                [vmem(SIZES[l] // NC, NC, slots, width // NX, width) for l in range(4)],
                [vmem(n, NX, width // NX, width) for n in (12, 8)],
                [vmem(SIZES[l] // NC, NC, *tile) for l in range(4)],
                pltpu.SMEM((1, 128), jnp.int32),
                pltpu.SMEM((32, 128), jnp.int32),
                vmem(levels, slots, part, width),
                vmem(*split),
                vmem(*split),
                vmem(NX, levels, slots, part, width),
                vmem(levels - 1, *tile, dtype=F32),
                vmem(levels, *tile),
                vmem(levels - 1, pair, width),
                vmem(sum(SIZES[1:4]) + 32, *tile),
                vmem(NX, 4, *tile),
                vmem(16, *tile),
                [vmem(n, *tile) for n in (8, 16, 32, 32)],
                vmem(2, *tile),
                vmem(32, NC, *tile),
                dma((8,)),
                dma((11,)),
                dma((11,)),
                dma((NX - 1,)),
                dma((NX - 1,)),
                dma((2, 4)),
                dma((2, 4)),
                dma((2, 4)),
                dma((2, 4)),
                dma((3,)),
                dma((3,)),
                dma((2,)),
                dma((2,)),
                dma((2, 4)),
                dma((2, 4)),
                dma((levels,)),
            ],
            compiler_params=pltpu.CompilerParams(
                collective_id=0, has_side_effects=True
            ),
        )(
            parent.T,
            live_count.T,
            rhs.reshape(levels, slots, NX, part, width),
            upd.reshape(levels, slots, NX, part, width),
            diag,
            lower,
            vinv,
            upper,
        )
        result = result.reshape(levels, NX, slots, part, width)
        return result.transpose(0, 2, 1, 3, 4).reshape(rhs.shape)

    return jax.shard_map(
        on_device,
        mesh=mesh,
        in_specs=(
            P(None, "grid", None, None),
            P("gz", None, "grid", None, None),
            P(None, "grid", None, None),
            P(None, "grid", None, None),
            P(None, "grid", None, None),
            P(None, "grid", None, None),
            P(None, "grid"),
            P(None, "grid"),
        ),
        out_specs=P(None, "grid", None, None),
        check_vma=False,
    )
```

```python
import functools

import jax
import jax.numpy as jnp
from jax import lax
from jax.experimental import pallas as pl
from jax.experimental.pallas import tpu as pltpu
from jax.sharding import PartitionSpec as P

MESH = pl.DeviceIdType.MESH
F32 = jnp.float32
BF16 = jnp.bfloat16
NX, NY, NZ, NC = 4, 4, 8, 2
LEVELS = 6
CHIPS_Z = (2, 4, 8, 8, 8)
CHIPS_Y = (1, 1, 1, 2, 4)
SIZES = tuple(NC * a * b for a, b in zip(CHIPS_Z, CHIPS_Y))


def ring(k, n):
    return min(k, n - k)


def offsets(mz, my, cores):
    every = [
        (dy, dz, dc) for dy in range(my) for dz in range(mz) for dc in range(cores)
    ]
    every.sort(key=lambda o: -(ring(o[0], NY) + ring(o[1], NZ)))
    return [o for o in every if o != (0, 0, 0)]


def kernel(
    parent_hbm,
    live_hbm,
    rhs,
    upd,
    diag_hbm,
    lower_hbm,
    vinv_hbm,
    upper_hbm,
    out,
    parent,
    live_count,
    diag,
    lower,
    vinv,
    upper,
    ml,
    uv_own,
    uv_part,
    tabs,
    picks,
    ftabs,
    ids_own,
    ids,
    rhs_own,
    rhs_first,
    upd_first,
    upd_all,
    fv,
    sol,
    chain,
    build,
    build0,
    in0,
    ins,
    mate,
    top_tab,
    load_sem,
    send,
    recv,
    rs_send,
    rs_recv,
    tab_send,
    tab_recv,
    ring_send,
    ring_recv,
    swap_send,
    swap_recv,
    pick_send,
    pick_recv,
    f_send,
    f_recv,
    own_sem,
):
    x = lax.axis_index("gz")
    g = lax.axis_index("grid")
    y, z, c = g // (NZ * NC), lax.rem(g // NC, NZ), lax.rem(g, NC)

    zs = {m: [z // m * m + lax.rem(z + k, m) for k in range(m)] for m in (2, 4, 8)}
    ys = {m: [y // m * m + lax.rem(y + k, m) for k in range(m)] for m in (1, 2, 4)}
    cs = [c, 1 - c]
    xs = [lax.rem(x + k, NX) for k in range(NX)]

    def at(off, mz, my):
        dy, dz, dc = off
        return (ys[my][dy] * NZ + zs[mz][dz]) * NC + cs[dc]

    def remote(src, dst, s, r, gx, gg):
        return pltpu.make_async_remote_copy(
            src_ref=src,
            dst_ref=dst,
            send_sem=s,
            recv_sem=r,
            device_id=(gx, gg),
            device_id_type=MESH,
        )

    def wait(view, sem):
        pltpu.make_async_copy(view, view, sem).wait()

    barrier = pltpu.get_barrier_semaphore()
    near = [(k, g) for k in xs[1:]]
    near += [(k, at(o, 2, 1)) for k in xs for o in offsets(2, 1, 2)]
    near += [(x, at((dy, 0, 0), 8, 4)) for dy in (1, 3)]
    far = [(0, dz, dc) for dz in (1, 2, 6, 7) for dc in (0, 1)]
    for gx, gg in near:
        pl.semaphore_signal(barrier, inc=1, device_id=(gx, gg), device_id_type=MESH)
    for o in far:
        pl.semaphore_signal(
            barrier, inc=1, device_id=(x, at(o, 8, 4)), device_id_type=MESH
        )

    loads = [
        pltpu.make_async_copy(upd.at[0], upd_first, load_sem.at[0]),
        pltpu.make_async_copy(rhs.at[0], rhs_first, load_sem.at[1]),
        pltpu.make_async_copy(diag_hbm.at[0], diag.at[0], load_sem.at[2]),
        pltpu.make_async_copy(lower_hbm.at[0], lower.at[0], load_sem.at[3]),
        pltpu.make_async_copy(vinv_hbm, vinv, load_sem.at[4]),
        pltpu.make_async_copy(upper_hbm, upper, load_sem.at[5]),
        pltpu.make_async_copy(rhs.at[:, :, x], rhs_own, load_sem.at[6]),
        pltpu.make_async_copy(upd.at[:, :, x], upd_all.at[0], load_sem.at[7]),
        pltpu.make_async_copy(
            diag_hbm.at[pl.ds(1, LEVELS - 1)],
            diag.at[pl.ds(1, LEVELS - 1)],
            load_sem.at[8],
        ),
        pltpu.make_async_copy(
            lower_hbm.at[pl.ds(1, LEVELS - 2)],
            lower.at[pl.ds(1, LEVELS - 2)],
            load_sem.at[9],
        ),
    ]
    ints = [
        pltpu.make_async_copy(parent_hbm, parent, load_sem.at[10]),
        pltpu.make_async_copy(live_hbm, live_count, load_sem.at[11]),
    ]
    for copy in ints + loads:
        copy.start()
    for copy in ints:
        copy.wait()
    for l in range(LEVELS - 1):
        for s in range(2):
            ids_own[0, 2 * l + s] = parent[s, l]

    row = lax.broadcasted_iota(jnp.int32, (16, 128), 0)
    slotrow = row // 8

    def spread(v, half):
        rows = lax.broadcasted_iota(jnp.int32, v.shape, 0)
        zero = jnp.zeros_like(v)
        return jnp.concatenate(
            [jnp.where(rows < half, v, zero), jnp.where(rows < half, zero, v)], axis=1
        ).astype(BF16)

    def live_of(l, rows=16):
        slot = lax.broadcasted_iota(jnp.int32, (rows, 128), 0) // (rows // 2)
        return (slot < live_count[0, l]).astype(F32)

    def dot(a, b):
        return jnp.dot(a, b, preferred_element_type=F32)

    def mats(ref, l):
        return ref[l].reshape(256, 128)

    def twice(v):
        return jnp.concatenate([v, v], axis=0)

    def target(p, n):
        return lax.rem(p, 2 * n) - slotrow

    def product(a, b, dst, l):
        for s in range(2):
            dst[l, pl.ds(128 * s, 128), :] = dot(a[l, s], b[l, s]).astype(BF16)

    for k in range(4):
        loads[k].wait()
    first = rhs_first[...].astype(F32).reshape(64, 128) * (x == 0).astype(F32)
    first = first - upd_first[...].astype(F32).reshape(64, 128)
    f0 = dot(spread(first, 32), mats(diag, 0)) * live_of(0, 64)
    sent = dot(spread(f0, 32), mats(lower, 0))
    off0 = [(0, 0, 0)] + offsets(2, 1, 2)
    rels = [lax.rem(at(o, 2, 1), 4) for o in off0]
    pa, pb = target(parent[0, 0], 4), target(parent[1, 0], 4)
    for q in range(NX):
        a = twice(sent[8 * q : 8 * q + 8])
        b = twice(sent[32 + 8 * q : 40 + 8 * q])
        zero = jnp.zeros_like(a)
        for k, rel in enumerate(rels):
            build0[q, k] = (
                jnp.where(pa == 2 * rel, a, zero) + jnp.where(pb == 2 * rel, b, zero)
            ).astype(BF16)

    pl.semaphore_wait(barrier, len(near) + len(far))

    for dx in (2, 1, 3, 0):
        for k, o in enumerate(off0):
            if dx or k:
                remote(
                    build0.at[xs[dx], k],
                    in0.at[4 * dx + k],
                    send.at[0],
                    recv.at[0],
                    xs[dx],
                    at(o, 2, 1),
                ).start()
    rs = [
        remote(
            upd.at[:, :, xs[k]],
            upd_all.at[k],
            rs_send.at[k - 1],
            rs_recv.at[k - 1],
            xs[k],
            g,
        )
        for k in range(1, NX)
    ]
    for copy in rs:
        copy.start()

    for k in range(4, 10):
        loads[k].wait()
    partner = at((0, 0, 1), 2, 1)
    part = pl.ds(32 * x, 32)
    up_row = lax.rem(y, 2)
    homes = [lax.rem(z, 2), lax.rem(z, 4), z, up_row * NZ + z]

    for l in (1, 2, 3, 4):
        for s in range(2):
            live = (s < live_count[0, l]).astype(F32)
            quarter = (dot(upper[l, s, part, :], vinv[l, s]) * live).astype(BF16)
            uv_part[l - 1, s] = quarter
            tabs[l - 1][homes[l - 1], c, s] = quarter

    def table_direct(l):
        nz = CHIPS_Z[l - 1]
        for o in offsets(nz, 1, 1):
            remote(
                uv_part.at[l - 1],
                tabs[l - 1].at[homes[l - 1], c],
                tab_send.at[0, l - 1],
                tab_recv.at[0, l - 1],
                x,
                at(o, nz, 1),
            ).start()

    def direct_view(l):
        return tabs[l - 1].at[pl.ds(0, CHIPS_Z[l - 1] - 1), 0]

    def table_ring(step):
        for i, first in ((0, 0), (1, up_row * NZ)):
            tab = tabs[2 + i]
            if step == 3:
                moves = [(z, (0, 4, 0))]
            else:
                moves = [
                    (lax.rem(z + NZ - step, NZ), (0, 1, 0)),
                    (lax.rem(z + step, NZ), (0, 7, 0)),
                ]
            for block, o in moves:
                remote(
                    tab.at[first + block, c] if step else uv_part.at[2 + i],
                    tab.at[first + block, c],
                    ring_send.at[i, step],
                    ring_recv.at[i, step],
                    x,
                    at(o, 8, 1),
                ).start()

    def ring_view(i, step):
        return tabs[2 + i].at[pl.ds(0, 1 if step == 3 else 2), 0]

    def ring_wait(step):
        for i in range(2):
            wait(ring_view(i, step), ring_recv.at[i, step])

    swaps = ((0, 1, 7), (2, 6), (3, 5, 4))

    def rows_swap(step):
        for k in swaps[step]:
            block = tabs[3].at[up_row * NZ + zs[8][k], c]
            remote(
                block,
                block,
                swap_send.at[step],
                swap_recv.at[step],
                x,
                at((1, 0, 0), 8, 2),
            ).start()

    def rows_view(step):
        return tabs[3].at[pl.ds(0, len(swaps[step])), 0]

    def core_swap(l):
        tab = tabs[l - 1]
        remote(
            tab.at[:, c],
            tab.at[:, c],
            tab_send.at[1, l - 1],
            tab_recv.at[1, l - 1],
            x,
            partner,
        ).start()

    def core_view(l):
        return tabs[l - 1].at[:, 0]

    def pick_share(i):
        for k in (2, 1, 3):
            remote(
                picks[i].at[:, x],
                picks[i].at[:, x],
                pick_send.at[i],
                pick_recv.at[i],
                xs[k],
                g,
            ).start()

    def pick_view(i):
        return picks[i].at[:, pl.ds(0, NX - 1)]

    def f_share(l):
        nz, ny = CHIPS_Z[l - 1], CHIPS_Y[l - 1]
        tab = ftabs[l - 1]
        tab[homes[l - 1], c] = fv[l].astype(BF16)
        for o in offsets(nz, ny, 1):
            remote(
                tab.at[homes[l - 1], c],
                tab.at[homes[l - 1], c],
                f_send.at[0, l - 1],
                f_recv.at[0, l - 1],
                x,
                at(o, nz, ny),
            ).start()

    def f_view(l):
        return ftabs[l - 1].at[pl.ds(0, SIZES[l - 1] // NC - 1), 0]

    def f_swap(l):
        wait(f_view(l), f_recv.at[0, l - 1])
        tab = ftabs[l - 1]
        remote(
            tab.at[:, c],
            tab.at[:, c],
            f_send.at[1, l - 1],
            f_recv.at[1, l - 1],
            x,
            partner,
        ).start()

    def f_wait(l):
        wait(ftabs[l - 1].at[:, 0], f_recv.at[1, l - 1])

    def f_tile(l, p):
        return half(ftabs[l - 1][p // 4, lax.rem(p // 2, 2)], p)

    def half(t, p):
        t = t.astype(F32)
        return jnp.where(lax.rem(p, 2) == 0, t[:8], t[8:])

    def forward(l, total):
        fwd = dot(spread(total, 8), mats(diag, l)) * live_of(l)
        fv[l] = dot(spread(fwd, 8), mats(vinv, l)) * live_of(l)

    def base(l):
        total = rhs_own[l].astype(F32).reshape(16, 128)
        for k in range(NX):
            total = total - upd_all[k, l].astype(F32).reshape(16, 128)
        return total

    table_direct(1)
    table_ring(0)
    product(diag, lower, ml, 1)
    for copy in rs:
        copy.wait_recv()
    bases = base(1)
    wait(in0.at[pl.ds(1, 15)], recv.at[0])
    incoming = build0[x, 0].astype(F32)
    for k in range(1, 16):
        incoming = incoming + in0[k].astype(F32)

    for l in (1, 2, 3):
        n, mz, my = SIZES[l], CHIPS_Z[l], CHIPS_Y[l]
        total = bases - incoming
        sent = dot(spread(total, 8), ml[l]) * live_of(l)
        a, b = twice(sent[:8]), twice(sent[8:])
        zero = jnp.zeros_like(a)
        pa, pb = target(parent[0, l], n), target(parent[1, l], n)

        def tile(rel):
            return (
                jnp.where(pa == 2 * rel, a, zero) + jnp.where(pb == 2 * rel, b, zero)
            ).astype(BF16)

        offs = offsets(mz, my, 2)
        goals = [at(o, mz, my) for o in offs]
        start = sum(SIZES[1:l])
        for k, goal in enumerate(goals):
            build[start + k] = tile(lax.rem(goal, n))
        for k, goal in enumerate(goals):
            remote(
                build.at[start + k], ins[l - 1].at[k], send.at[l], recv.at[l], x, goal
            ).start()
        own = tile(lax.rem(g, n)).astype(F32)

        forward(l, total)
        f_share(l)
        if l == 1:
            table_direct(2)
            ring_wait(0)
            table_ring(1)
            rows_swap(0)
            forward(0, base(0))
        if l == 2:
            mine = lax.rem(g, 32)
            for s in range(10):
                ids[mine, s] = ids_own[0, s]
            for o in offsets(8, 1, 2):
                remote(
                    ids_own,
                    ids.at[pl.ds(mine, 1)],
                    send.at[8],
                    recv.at[8],
                    x,
                    at(o, 8, 1),
                ).start()
            ring_wait(1)
            table_ring(2)
            table_ring(3)
            rows_swap(1)
            for j in (1, 2):
                wait(direct_view(j), tab_recv.at[0, j - 1])
                core_swap(j)
        if l == 3:
            ring_wait(2)
            ring_wait(3)
            rows_swap(2)
            core_swap(3)
            wait(ids.at[pl.ds(0, 15)], recv.at[8])
            half_ids = ids.at[pl.ds(16 * up_row, 16)]
            remote(
                half_ids, half_ids, send.at[7], recv.at[7], x, at((1, 0, 0), 8, 2)
            ).start()
        product(diag, lower, ml, l + 1)
        product(upper, vinv, uv_own, l)
        if l == 3:
            for j in (1, 2, 3):
                wait(core_view(j), tab_recv.at[1, j - 1])
            wait(half_ids, recv.at[7])
            chains = []
            for k in range(4):
                for s in range(2):
                    path = {}
                    p = parent[s, k]
                    for j in range(k + 1, 5):
                        n = SIZES[j - 1]
                        path[j] = lax.rem(p, 2 * n)
                        p = ids[
                            lax.rem(path[j] // 2, n) + (g // n * n - g // 32 * 32),
                            2 * j + lax.rem(path[j], 2),
                        ]
                    path[5] = lax.rem(p, 128)
                    chains.append(path)
            places = {}
            for k in range(3):
                for s in range(2):
                    for j in range(k + 1, 4):
                        p = chains[2 * k + s][j]
                        places[k, s, j] = len(places)
                        picks[0][places[k, s, j], x] = tabs[j - 1][
                            p // 4, lax.rem(p // 2, 2), lax.rem(p, 2)
                        ]
            pick_share(0)
        bases = base(l + 1)
        wait(ins[l - 1].at[pl.ds(0, n - 1)], recv.at[l])
        incoming = own
        for k in range(n - 1):
            incoming = incoming + ins[l - 1][k].astype(F32)

    total = bases - incoming
    sent = dot(spread(total, 8), ml[4]) * live_of(4)
    mate[0] = sent.astype(BF16)
    remote(mate.at[0], mate.at[1], send.at[5], recv.at[5], x, partner).start()
    pa, pb = target(parent[0, 4], 64), target(parent[1, 4], 64)
    other = lax.rem(partner, 32)
    pc, pd = target(ids[other, 8], 64), target(ids[other, 9], 64)
    offs = offsets(8, 4, 1)
    goals = [at(o, 8, 4) for o in offs]
    a, b = twice(sent[:8]), twice(sent[8:])
    bases = base(5)
    wait(mate.at[1], recv.at[5])
    third = mate[1].astype(F32)
    d, e = twice(third[:8]), twice(third[8:])
    zero = jnp.zeros_like(a)

    def tile4(goal):
        return (
            jnp.where(pa == 2 * goal, a, zero)
            + jnp.where(pb == 2 * goal, b, zero)
            + jnp.where(pc == 2 * goal, d, zero)
            + jnp.where(pd == 2 * goal, e, zero)
        ).astype(BF16)

    start = sum(SIZES[1:4])
    for k, goal in enumerate(goals):
        build[start + k] = tile4(goal)
    for k, goal in enumerate(goals):
        remote(
            build.at[start + k], ins[3].at[k], send.at[4], recv.at[4], x, goal
        ).start()
    own = tile4(g).astype(F32)
    for j in (1, 2, 3):
        f_swap(j)
    for step in range(3):
        wait(rows_view(step), swap_recv.at[step])
    core_swap(4)
    forward(4, total)
    f_share(4)
    product(upper, vinv, uv_own, 4)
    product(upper, vinv, uv_own, 0)
    wait(core_view(4), tab_recv.at[1, 3])
    for k in range(4):
        for s in range(2):
            p = chains[2 * k + s][4]
            picks[1][2 * k + s, x] = tabs[3][p // 4, lax.rem(p // 2, 2), lax.rem(p, 2)]
    pick_share(1)

    wait(pick_view(0), pick_recv.at[0])
    for j in (1, 2, 3):
        f_wait(j)
    for k in range(4):
        consts = []
        for s in range(2):
            path = chains[2 * k + s]
            m = const = None
            for j in range(3, k - 1, -1):
                if j == k:
                    u = uv_own[k, pl.ds(128 * s, 128), :]
                    f = fv[k, pl.ds(8 * s, 8), :]
                else:
                    u = picks[0][places[k, s, j]].reshape(128, 128)
                    f = f_tile(j, path[j])
                if m is None:
                    m, const = u, f
                else:
                    const = f - dot(const.astype(BF16), u)
                    m = dot(m, u).astype(BF16)
            chain[k, pl.ds(128 * s, 128), :] = m
            consts.append(const)
        fv[k] = jnp.concatenate(consts, axis=0)
    wait(ins[3].at[pl.ds(0, 31)], recv.at[4])
    incoming = own
    for k in range(31):
        incoming = incoming + ins[3][k].astype(F32)

    fwd = dot(spread(bases - incoming, 8), mats(diag, 5)) * live_of(5)
    answer = (dot(spread(fwd, 8), mats(vinv, 5)) * live_of(5)).astype(BF16)
    sol[5] = answer.reshape(2, 8, 128)

    def share(first, count):
        span = pl.ds(first, count)
        for k in (2, 1, 3):
            remote(
                sol.at[span], out.at[span, :, x], send.at[9], recv.at[9], xs[k], g
            ).start()
        pltpu.make_async_copy(
            sol.at[span], out.at[span, :, x], own_sem.at[first]
        ).start()

    chip = y * NZ + z
    for o in offs:
        remote(
            sol.at[5], top_tab.at[chip, c], send.at[6], recv.at[6], x, at(o, 8, 4)
        ).start()
    top_tab[chip, c] = sol[5]
    share(5, 1)

    f_swap(4)
    wait(pick_view(1), pick_recv.at[1])
    f_wait(4)
    for k in range(4):
        sign = 1 if k % 2 == 0 else -1
        ends = [chains[2 * k + s][4] for s in range(2)]
        f = jnp.concatenate([f_tile(4, p) for p in ends], axis=0)
        fv[k] = fv[k] + sign * dot(spread(f, 8), chain[k])
        for s in range(2):
            span = pl.ds(128 * s, 128)
            u = picks[1][2 * k + s].reshape(128, 128)
            chain[k, span, :] = dot(u, chain[k, span, :]).astype(BF16)
    for s in range(2):
        chain[4, pl.ds(128 * s, 128), :] = uv_own[4, pl.ds(128 * s, 128), :]

    wait(top_tab.at[pl.ds(0, 31), 0], recv.at[6])
    remote(
        top_tab.at[:, c], top_tab.at[:, c], send.at[10], recv.at[10], x, partner
    ).start()
    wait(top_tab.at[:, 0], recv.at[10])
    for k in range(5):
        if k < 4:
            ends = [chains[2 * k + s][5] for s in range(2)]
        else:
            ends = [lax.rem(parent[s, 4], 128) for s in range(2)]
        above = jnp.concatenate(
            [
                top_tab[p // 4, lax.rem(p // 2, 2), lax.rem(p, 2)].astype(F32)
                for p in ends
            ],
            axis=0,
        )
        low = dot(spread(above, 8), chain[k])
        value = fv[k] + low if k % 2 == 1 else fv[k] - low
        sol[k] = (value * live_of(k)).astype(BF16).reshape(2, 8, 128)
    share(0, 5)

    wait(in0.at[pl.ds(1, 15)], send.at[0])
    for copy in rs:
        copy.wait_send()
    for l in (1, 2, 3):
        wait(ins[l - 1].at[pl.ds(0, SIZES[l] - 1)], send.at[l])
        if l < 3:
            wait(direct_view(l), tab_send.at[0, l - 1])
    for step in range(4):
        for i in range(2):
            wait(ring_view(i, step), ring_send.at[i, step])
    for step in range(3):
        wait(rows_view(step), swap_send.at[step])
    for l in (1, 2, 3, 4):
        wait(core_view(l), tab_send.at[1, l - 1])
        wait(f_view(l), f_send.at[0, l - 1])
        wait(ftabs[l - 1].at[:, 0], f_send.at[1, l - 1])
    for i in range(2):
        wait(pick_view(i), pick_send.at[i])
    wait(ins[3].at[pl.ds(0, 31)], send.at[4])
    wait(mate.at[0], send.at[5])
    wait(top_tab.at[pl.ds(0, 31), 0], send.at[6])
    wait(half_ids, send.at[7])
    wait(ids.at[pl.ds(0, 15)], send.at[8])
    wait(top_tab.at[:, 0], send.at[10])
    for first, count in ((5, 1), (0, 5)):
        span = pl.ds(first, count)
        pltpu.make_async_copy(
            sol.at[span], out.at[span, :, x], own_sem.at[first]
        ).wait()
    whole = out.at[:, :, pl.ds(0, NX - 1)]
    wait(whole, send.at[9])
    wait(whole, recv.at[9])


def solution(mesh):
    def on_device(rhs, upd, diag, lower, vinv, upper, parent, live_count):
        levels, slots, rows, width = rhs.shape
        part = rows // NX
        hbm = pl.BlockSpec(memory_space=pl.ANY)
        dma = pltpu.SemaphoreType.DMA
        pair = slots * width
        tile = (slots * part, width)
        split = (slots, NX, part, width)

        def vmem(*shape, dtype=BF16):
            return pltpu.VMEM(shape, dtype)

        result = pl.pallas_call(
            kernel,
            out_shape=pltpu.VMEM((levels,) + split, BF16),
            in_specs=[hbm] * 8,
            out_specs=hbm,
            scratch_shapes=[
                pltpu.SMEM(parent.shape[::-1], jnp.int32),
                pltpu.SMEM(live_count.shape[::-1], jnp.int32),
                vmem(*diag.shape),
                vmem(*lower.shape),
                vmem(*vinv.shape),
                vmem(*upper.shape),
                vmem(levels - 1, pair, width),
                vmem(levels - 1, pair, width),
                vmem(4, slots, width // NX, width),
                [vmem(SIZES[l] // NC, NC, slots, width // NX, width) for l in range(4)],
                [vmem(n, NX, width // NX, width) for n in (12, 8)],
                [vmem(SIZES[l] // NC, NC, *tile) for l in range(4)],
                pltpu.SMEM((1, 128), jnp.int32),
                pltpu.SMEM((32, 128), jnp.int32),
                vmem(levels, slots, part, width),
                vmem(*split),
                vmem(*split),
                vmem(NX, levels, slots, part, width),
                vmem(levels - 1, *tile, dtype=F32),
                vmem(levels, slots, part, width),
                vmem(levels - 1, pair, width),
                vmem(sum(SIZES[1:4]) + 32, *tile),
                vmem(NX, 4, *tile),
                vmem(16, *tile),
                [vmem(n, *tile) for n in (8, 16, 32, 32)],
                vmem(2, *tile),
                vmem(32, NC, slots, part, width),
                dma((12,)),
                dma((11,)),
                dma((11,)),
                dma((NX - 1,)),
                dma((NX - 1,)),
                dma((2, 4)),
                dma((2, 4)),
                dma((2, 4)),
                dma((2, 4)),
                dma((3,)),
                dma((3,)),
                dma((2,)),
                dma((2,)),
                dma((2, 4)),
                dma((2, 4)),
                dma((levels,)),
            ],
            compiler_params=pltpu.CompilerParams(
                collective_id=0, has_side_effects=True
            ),
        )(
            parent.T,
            live_count.T,
            rhs.reshape(levels, slots, NX, part, width),
            upd.reshape(levels, slots, NX, part, width),
            diag,
            lower,
            vinv,
            upper,
        )
        return result.reshape(rhs.shape)

    return jax.shard_map(
        on_device,
        mesh=mesh,
        in_specs=(
            P(None, "grid", None, None),
            P("gz", None, "grid", None, None),
            P(None, "grid", None, None),
            P(None, "grid", None, None),
            P(None, "grid", None, None),
            P(None, "grid", None, None),
            P(None, "grid"),
            P(None, "grid"),
        ),
        out_specs=P(None, "grid", None, None),
        check_vma=False,
    )
```

```python
import functools

import jax
import jax.numpy as jnp
from jax import lax
from jax.experimental import pallas as pl
from jax.experimental.pallas import tpu as pltpu
from jax.sharding import PartitionSpec as P

MESH = pl.DeviceIdType.MESH
F32 = jnp.float32
BF16 = jnp.bfloat16
NX, NY, NZ, NC = 4, 4, 8, 2
LEVELS = 6
CHIPS_Z = (2, 4, 8, 8, 8)
CHIPS_Y = (1, 1, 1, 2, 4)
SIZES = tuple(NC * a * b for a, b in zip(CHIPS_Z, CHIPS_Y))


def ring(k, n):
    return min(k, n - k)


def offsets(mz, my, cores):
    every = [
        (dy, dz, dc) for dy in range(my) for dz in range(mz) for dc in range(cores)
    ]
    every.sort(key=lambda o: -(ring(o[0], NY) + ring(o[1], NZ)))
    return [o for o in every if o != (0, 0, 0)]


def kernel(
    parent_hbm,
    live_hbm,
    rhs,
    upd,
    diag_hbm,
    lower_hbm,
    vinv_hbm,
    upper_hbm,
    out,
    parent,
    live_count,
    diag,
    lower,
    vinv,
    upper,
    ml,
    uv_own,
    uv_part,
    tabs,
    picks,
    ftabs,
    ids_own,
    ids_mate,
    ids,
    rhs_own,
    rhs_first,
    upd_first,
    upd_all,
    fv,
    sol,
    chain,
    build,
    build0,
    in0,
    ins,
    mate,
    top_tab,
    mate_send,
    mate_recv,
    load_sem,
    send,
    recv,
    rs_send,
    rs_recv,
    tab_send,
    tab_recv,
    ring_send,
    ring_recv,
    swap_send,
    swap_recv,
    pick_send,
    pick_recv,
    f_send,
    f_recv,
    own_sem,
):
    x = lax.axis_index("gz")
    g = lax.axis_index("grid")
    y, z, c = g // (NZ * NC), lax.rem(g // NC, NZ), lax.rem(g, NC)

    zs = {m: [z // m * m + lax.rem(z + k, m) for k in range(m)] for m in (2, 4, 8)}
    ys = {m: [y // m * m + lax.rem(y + k, m) for k in range(m)] for m in (1, 2, 4)}
    cs = [c, 1 - c]
    xs = [lax.rem(x + k, NX) for k in range(NX)]

    def at(off, mz, my):
        dy, dz, dc = off
        return (ys[my][dy] * NZ + zs[mz][dz]) * NC + cs[dc]

    def remote(src, dst, s, r, gx, gg):
        return pltpu.make_async_remote_copy(
            src_ref=src,
            dst_ref=dst,
            send_sem=s,
            recv_sem=r,
            device_id=(gx, gg),
            device_id_type=MESH,
        )

    def wait(view, sem):
        pltpu.make_async_copy(view, view, sem).wait()

    barrier = pltpu.get_barrier_semaphore()
    near = [(k, g) for k in xs[1:]]
    near += [(k, at(o, 2, 1)) for k in xs for o in offsets(2, 1, 2)]
    near += [(x, at((dy, 0, 0), 8, 4)) for dy in (1, 3)]
    far = [(0, dz, dc) for dz in (1, 2, 6, 7) for dc in (0, 1)]
    for gx, gg in near:
        pl.semaphore_signal(barrier, inc=1, device_id=(gx, gg), device_id_type=MESH)
    for o in far:
        pl.semaphore_signal(
            barrier, inc=1, device_id=(x, at(o, 8, 4)), device_id_type=MESH
        )

    loads = [
        pltpu.make_async_copy(upd.at[0], upd_first, load_sem.at[0]),
        pltpu.make_async_copy(rhs.at[0], rhs_first, load_sem.at[1]),
        pltpu.make_async_copy(diag_hbm.at[0], diag.at[0], load_sem.at[2]),
        pltpu.make_async_copy(lower_hbm.at[0], lower.at[0], load_sem.at[3]),
        pltpu.make_async_copy(vinv_hbm, vinv, load_sem.at[4]),
        pltpu.make_async_copy(upper_hbm, upper, load_sem.at[5]),
        pltpu.make_async_copy(rhs.at[:, :, x], rhs_own, load_sem.at[6]),
        pltpu.make_async_copy(upd.at[:, :, x], upd_all.at[0], load_sem.at[7]),
        pltpu.make_async_copy(
            diag_hbm.at[pl.ds(1, LEVELS - 1)],
            diag.at[pl.ds(1, LEVELS - 1)],
            load_sem.at[8],
        ),
        pltpu.make_async_copy(
            lower_hbm.at[pl.ds(1, LEVELS - 2)],
            lower.at[pl.ds(1, LEVELS - 2)],
            load_sem.at[9],
        ),
    ]
    ints = [
        pltpu.make_async_copy(parent_hbm, parent, load_sem.at[10]),
        pltpu.make_async_copy(live_hbm, live_count, load_sem.at[11]),
    ]
    for copy in ints + loads:
        copy.start()
    for copy in ints:
        copy.wait()
    for l in range(LEVELS - 1):
        for s in range(2):
            ids_own[0, 2 * l + s] = parent[s, l]

    row = lax.broadcasted_iota(jnp.int32, (16, 128), 0)
    slotrow = row // 8

    def spread(v, half):
        rows = lax.broadcasted_iota(jnp.int32, v.shape, 0)
        zero = jnp.zeros_like(v)
        return jnp.concatenate(
            [jnp.where(rows < half, v, zero), jnp.where(rows < half, zero, v)], axis=1
        ).astype(BF16)

    def live_of(l, rows=16):
        slot = lax.broadcasted_iota(jnp.int32, (rows, 128), 0) // (rows // 2)
        return (slot < live_count[0, l]).astype(F32)

    def dot(a, b):
        return jnp.dot(a, b, preferred_element_type=F32)

    def mats(ref, l):
        return ref[l].reshape(256, 128)

    def twice(v):
        return jnp.concatenate([v, v], axis=0)

    def target(p, n):
        return lax.rem(p, 2 * n) - slotrow

    def product(a, b, dst, l):
        for s in range(2):
            dst[l, pl.ds(128 * s, 128), :] = dot(a[l, s], b[l, s]).astype(BF16)

    for k in range(4):
        loads[k].wait()
    first = rhs_first[...].astype(F32).reshape(64, 128) * (x == 0).astype(F32)
    first = first - upd_first[...].astype(F32).reshape(64, 128)
    f0 = dot(spread(first, 32), mats(diag, 0)) * live_of(0, 64)
    sent = dot(spread(f0, 32), mats(lower, 0))
    off0 = [(0, 0, 0)] + offsets(2, 1, 2)
    rels = [lax.rem(at(o, 2, 1), 4) for o in off0]
    pa, pb = target(parent[0, 0], 4), target(parent[1, 0], 4)
    for q in range(NX):
        a = twice(sent[8 * q : 8 * q + 8])
        b = twice(sent[32 + 8 * q : 40 + 8 * q])
        zero = jnp.zeros_like(a)
        for k, rel in enumerate(rels):
            build0[q, k] = (
                jnp.where(pa == 2 * rel, a, zero) + jnp.where(pb == 2 * rel, b, zero)
            ).astype(BF16)

    pl.semaphore_wait(barrier, len(near) + len(far))

    for dx in (2, 1, 3, 0):
        for k, o in enumerate(off0):
            if dx or k:
                remote(
                    build0.at[xs[dx], k],
                    in0.at[4 * dx + k],
                    send.at[0],
                    recv.at[0],
                    xs[dx],
                    at(o, 2, 1),
                ).start()
    rs = [
        remote(
            upd.at[:, :, xs[k]],
            upd_all.at[k],
            rs_send.at[k - 1],
            rs_recv.at[k - 1],
            xs[k],
            g,
        )
        for k in range(1, NX)
    ]
    for copy in rs:
        copy.start()

    for k in range(4, 10):
        loads[k].wait()
    partner = at((0, 0, 1), 2, 1)
    part = pl.ds(32 * x, 32)
    up_row = lax.rem(y, 2)
    homes = [lax.rem(z, 2), lax.rem(z, 4), z, up_row * NZ + z]

    for l in (1, 2, 3, 4):
        for s in range(2):
            live = (s < live_count[0, l]).astype(F32)
            quarter = (dot(upper[l, s, part, :], vinv[l, s]) * live).astype(BF16)
            uv_part[l - 1, s] = quarter
            tabs[l - 1][homes[l - 1], c, s] = quarter

    def table_direct(l):
        nz = CHIPS_Z[l - 1]
        for o in offsets(nz, 1, 1):
            remote(
                uv_part.at[l - 1],
                tabs[l - 1].at[homes[l - 1], c],
                tab_send.at[0, l - 1],
                tab_recv.at[0, l - 1],
                x,
                at(o, nz, 1),
            ).start()

    def direct_view(l):
        return tabs[l - 1].at[pl.ds(0, CHIPS_Z[l - 1] - 1), 0]

    def table_ring(step):
        for i, first in ((0, 0), (1, up_row * NZ)):
            tab = tabs[2 + i]
            if step == 3:
                moves = [(z, (0, 4, 0))]
            else:
                moves = [
                    (lax.rem(z + NZ - step, NZ), (0, 1, 0)),
                    (lax.rem(z + step, NZ), (0, 7, 0)),
                ]
            for block, o in moves:
                remote(
                    tab.at[first + block, c] if step else uv_part.at[2 + i],
                    tab.at[first + block, c],
                    ring_send.at[i, step],
                    ring_recv.at[i, step],
                    x,
                    at(o, 8, 1),
                ).start()

    def ring_view(i, step):
        return tabs[2 + i].at[pl.ds(0, 1 if step == 3 else 2), 0]

    def ring_wait(step):
        for i in range(2):
            wait(ring_view(i, step), ring_recv.at[i, step])

    swaps = ((0, 1, 7), (2, 6), (3, 5, 4))

    def rows_swap(step):
        for k in swaps[step]:
            block = tabs[3].at[up_row * NZ + zs[8][k], c]
            remote(
                block,
                block,
                swap_send.at[step],
                swap_recv.at[step],
                x,
                at((1, 0, 0), 8, 2),
            ).start()

    def rows_view(step):
        return tabs[3].at[pl.ds(0, len(swaps[step])), 0]

    def core_swap(l):
        tab = tabs[l - 1]
        remote(
            tab.at[:, c],
            tab.at[:, c],
            tab_send.at[1, l - 1],
            tab_recv.at[1, l - 1],
            x,
            partner,
        ).start()

    def core_view(l):
        return tabs[l - 1].at[:, 0]

    def pick_share(i):
        for k in (2, 1, 3):
            remote(
                picks[i].at[:, x],
                picks[i].at[:, x],
                pick_send.at[i],
                pick_recv.at[i],
                xs[k],
                g,
            ).start()

    def pick_view(i):
        return picks[i].at[:, pl.ds(0, NX - 1)]

    def f_share(l):
        nz, ny = CHIPS_Z[l - 1], CHIPS_Y[l - 1]
        tab = ftabs[l - 1]
        tab[homes[l - 1], c] = fv[l].astype(BF16)
        for o in offsets(nz, ny, 1):
            remote(
                tab.at[homes[l - 1], c],
                tab.at[homes[l - 1], c],
                f_send.at[0, l - 1],
                f_recv.at[0, l - 1],
                x,
                at(o, nz, ny),
            ).start()

    def f_view(l):
        return ftabs[l - 1].at[pl.ds(0, SIZES[l - 1] // NC - 1), 0]

    def f_swap(l):
        wait(f_view(l), f_recv.at[0, l - 1])
        tab = ftabs[l - 1]
        remote(
            tab.at[:, c],
            tab.at[:, c],
            f_send.at[1, l - 1],
            f_recv.at[1, l - 1],
            x,
            partner,
        ).start()

    def f_wait(l):
        wait(ftabs[l - 1].at[:, 0], f_recv.at[1, l - 1])

    def f_tile(l, p):
        return half(ftabs[l - 1][p // 4, lax.rem(p // 2, 2)], p)

    def half(t, p):
        t = t.astype(F32)
        return jnp.where(lax.rem(p, 2) == 0, t[:8], t[8:])

    def forward(l, total):
        fwd = dot(spread(total, 8), mats(diag, l)) * live_of(l)
        fv[l] = dot(spread(fwd, 8), mats(vinv, l)) * live_of(l)

    def base(l):
        total = rhs_own[l].astype(F32).reshape(16, 128)
        for k in range(NX):
            total = total - upd_all[k, l].astype(F32).reshape(16, 128)
        return total

    remote(ids_own, ids_mate, send.at[5], recv.at[5], x, partner).start()
    product(diag, lower, ml, 1)
    table_direct(1)
    table_ring(0)
    for copy in rs:
        copy.wait_recv()
    bases = base(1)
    wait(in0.at[pl.ds(1, 15)], recv.at[0])
    incoming = build0[x, 0].astype(F32)
    for k in range(1, 16):
        incoming = incoming + in0[k].astype(F32)

    def mate_terms(l, sent):
        i = 2 * (l - 3)
        mate[i] = sent.astype(BF16)
        remote(
            mate.at[i], mate.at[i + 1], mate_send.at[l - 3], mate_recv.at[l - 3], x, partner
        ).start()
        wait(mate.at[i + 1], mate_recv.at[l - 3])
        theirs = mate[i + 1].astype(F32)
        return [
            (ids_mate[0, 2 * l], theirs[:8]),
            (ids_mate[0, 2 * l + 1], theirs[8:]),
        ]

    def masked(p, v, rel, n):
        return jnp.where(target(p, n) == 2 * rel, twice(v), jnp.zeros((16, 128), F32))

    for l in (1, 2, 3):
        n, mz, my = SIZES[l], CHIPS_Z[l], CHIPS_Y[l]
        total = bases - incoming
        sent = dot(spread(total, 8), ml[l]) * live_of(l)
        terms = [(parent[0, l], sent[:8]), (parent[1, l], sent[8:])]
        if l == 3:
            terms += mate_terms(l, sent)

        def tile(rel):
            return sum(masked(p, v, rel, n) for p, v in terms).astype(BF16)

        offs = offsets(mz, my, 1 if l == 3 else 2)
        goals = [at(o, mz, my) for o in offs]
        start = sum(SIZES[1:l])
        for k, goal in enumerate(goals):
            build[start + k] = tile(lax.rem(goal, n))
        for k, goal in enumerate(goals):
            remote(
                build.at[start + k], ins[l - 1].at[k], send.at[l], recv.at[l], x, goal
            ).start()
        own = tile(lax.rem(g, n)).astype(F32)

        forward(l, total)
        f_share(l)
        if l == 1:
            table_direct(2)
            ring_wait(0)
            table_ring(1)
            rows_swap(0)
            forward(0, base(0))
        if l == 2:
            wait(ids_mate, recv.at[5])
            mine = lax.rem(g, 32)
            for s in range(10):
                ids[mine, s] = ids_own[0, s]
            for o in offsets(8, 1, 2):
                remote(
                    ids_own,
                    ids.at[pl.ds(mine, 1)],
                    send.at[8],
                    recv.at[8],
                    x,
                    at(o, 8, 1),
                ).start()
            ring_wait(1)
            table_ring(2)
            table_ring(3)
            rows_swap(1)
            for j in (1, 2):
                wait(direct_view(j), tab_recv.at[0, j - 1])
                core_swap(j)
        if l == 3:
            wait(ids.at[pl.ds(0, 15)], recv.at[8])
            half_ids = ids.at[pl.ds(16 * up_row, 16)]
            remote(
                half_ids, half_ids, send.at[7], recv.at[7], x, at((1, 0, 0), 8, 2)
            ).start()
            ring_wait(2)
            ring_wait(3)
            rows_swap(2)
            core_swap(3)
        product(diag, lower, ml, l + 1)
        product(upper, vinv, uv_own, l)
        if l == 3:
            for j in (1, 2, 3):
                wait(core_view(j), tab_recv.at[1, j - 1])
            wait(half_ids, recv.at[7])
            chains = []
            for k in range(4):
                for s in range(2):
                    path = {}
                    p = parent[s, k]
                    for j in range(k + 1, 5):
                        n = SIZES[j - 1]
                        path[j] = lax.rem(p, 2 * n)
                        p = ids[
                            lax.rem(path[j] // 2, n) + (g // n * n - g // 32 * 32),
                            2 * j + lax.rem(path[j], 2),
                        ]
                    path[5] = lax.rem(p, 128)
                    chains.append(path)
            places = {}
            for k in range(3):
                for s in range(2):
                    for j in range(k + 1, 4):
                        p = chains[2 * k + s][j]
                        places[k, s, j] = len(places)
                        picks[0][places[k, s, j], x] = tabs[j - 1][
                            p // 4, lax.rem(p // 2, 2), lax.rem(p, 2)
                        ]
            pick_share(0)
        bases = base(l + 1)
        wait(ins[l - 1].at[pl.ds(0, len(goals))], recv.at[l])
        incoming = own
        for k in range(len(goals)):
            incoming = incoming + ins[l - 1][k].astype(F32)

    total = bases - incoming
    sent = dot(spread(total, 8), ml[4]) * live_of(4)
    terms = [(parent[0, 4], sent[:8]), (parent[1, 4], sent[8:])]
    offs = offsets(8, 4, 1)
    goals = [at(o, 8, 4) for o in offs]
    bases = base(5)
    terms += mate_terms(4, sent)

    def tile4(goal):
        return sum(masked(p, v, goal, 64) for p, v in terms).astype(BF16)

    start = sum(SIZES[1:4])
    for k, goal in enumerate(goals):
        build[start + k] = tile4(goal)
    for k, goal in enumerate(goals):
        remote(
            build.at[start + k], ins[3].at[k], send.at[4], recv.at[4], x, goal
        ).start()
    own = tile4(g).astype(F32)
    for j in (1, 2, 3):
        f_swap(j)
    for step in range(3):
        wait(rows_view(step), swap_recv.at[step])
    core_swap(4)
    forward(4, total)
    f_share(4)
    product(upper, vinv, uv_own, 4)
    product(upper, vinv, uv_own, 0)
    wait(core_view(4), tab_recv.at[1, 3])
    for k in range(4):
        for s in range(2):
            p = chains[2 * k + s][4]
            picks[1][2 * k + s, x] = tabs[3][p // 4, lax.rem(p // 2, 2), lax.rem(p, 2)]
    pick_share(1)

    wait(pick_view(0), pick_recv.at[0])
    for j in (1, 2, 3):
        f_wait(j)
    for k in range(4):
        consts = []
        for s in range(2):
            path = chains[2 * k + s]
            m = const = None
            for j in range(3, k - 1, -1):
                if j == k:
                    u = uv_own[k, pl.ds(128 * s, 128), :]
                    f = fv[k, pl.ds(8 * s, 8), :]
                else:
                    u = picks[0][places[k, s, j]].reshape(128, 128)
                    f = f_tile(j, path[j])
                if m is None:
                    m, const = u, f
                else:
                    const = f - dot(const.astype(BF16), u)
                    m = dot(m, u).astype(BF16)
            chain[k, pl.ds(128 * s, 128), :] = m
            consts.append(const)
        fv[k] = jnp.concatenate(consts, axis=0)
    wait(ins[3].at[pl.ds(0, 31)], recv.at[4])
    incoming = own
    for k in range(31):
        incoming = incoming + ins[3][k].astype(F32)

    fwd = dot(spread(bases - incoming, 8), mats(diag, 5)) * live_of(5)
    answer = (dot(spread(fwd, 8), mats(vinv, 5)) * live_of(5)).astype(BF16)
    sol[5] = answer.reshape(2, 8, 128)

    def share(first, count):
        span = pl.ds(first, count)
        for k in (2, 1, 3):
            remote(
                sol.at[span], out.at[span, :, x], send.at[9], recv.at[9], xs[k], g
            ).start()
        pltpu.make_async_copy(
            sol.at[span], out.at[span, :, x], own_sem.at[first]
        ).start()

    chip = y * NZ + z
    for o in offs:
        remote(
            sol.at[5], top_tab.at[chip, c], send.at[6], recv.at[6], x, at(o, 8, 4)
        ).start()
    top_tab[chip, c] = sol[5]
    share(5, 1)

    f_swap(4)
    wait(pick_view(1), pick_recv.at[1])
    f_wait(4)
    for k in range(4):
        sign = 1 if k % 2 == 0 else -1
        ends = [chains[2 * k + s][4] for s in range(2)]
        f = jnp.concatenate([f_tile(4, p) for p in ends], axis=0)
        fv[k] = fv[k] + sign * dot(spread(f, 8), chain[k])
        for s in range(2):
            span = pl.ds(128 * s, 128)
            u = picks[1][2 * k + s].reshape(128, 128)
            chain[k, span, :] = dot(u, chain[k, span, :]).astype(BF16)
    for s in range(2):
        chain[4, pl.ds(128 * s, 128), :] = uv_own[4, pl.ds(128 * s, 128), :]

    wait(top_tab.at[pl.ds(0, 31), 0], recv.at[6])
    remote(
        top_tab.at[:, c], top_tab.at[:, c], send.at[10], recv.at[10], x, partner
    ).start()
    wait(top_tab.at[:, 0], recv.at[10])
    for k in range(5):
        if k < 4:
            ends = [chains[2 * k + s][5] for s in range(2)]
        else:
            ends = [lax.rem(parent[s, 4], 128) for s in range(2)]
        above = jnp.concatenate(
            [
                top_tab[p // 4, lax.rem(p // 2, 2), lax.rem(p, 2)].astype(F32)
                for p in ends
            ],
            axis=0,
        )
        low = dot(spread(above, 8), chain[k])
        value = fv[k] + low if k % 2 == 1 else fv[k] - low
        sol[k] = (value * live_of(k)).astype(BF16).reshape(2, 8, 128)
    share(0, 5)

    wait(in0.at[pl.ds(1, 15)], send.at[0])
    for copy in rs:
        copy.wait_send()
    for l in (1, 2):
        wait(ins[l - 1].at[pl.ds(0, SIZES[l] - 1)], send.at[l])
        wait(direct_view(l), tab_send.at[0, l - 1])
    wait(ins[2].at[pl.ds(0, 15)], send.at[3])
    for i in range(2):
        wait(mate.at[2 * i], mate_send.at[i])
    for step in range(4):
        for i in range(2):
            wait(ring_view(i, step), ring_send.at[i, step])
    for step in range(3):
        wait(rows_view(step), swap_send.at[step])
    for l in (1, 2, 3, 4):
        wait(core_view(l), tab_send.at[1, l - 1])
        wait(f_view(l), f_send.at[0, l - 1])
        wait(ftabs[l - 1].at[:, 0], f_send.at[1, l - 1])
    for i in range(2):
        wait(pick_view(i), pick_send.at[i])
    wait(ins[3].at[pl.ds(0, 31)], send.at[4])
    wait(ids_own, send.at[5])
    wait(top_tab.at[pl.ds(0, 31), 0], send.at[6])
    wait(half_ids, send.at[7])
    wait(ids.at[pl.ds(0, 15)], send.at[8])
    wait(top_tab.at[:, 0], send.at[10])
    for first, count in ((5, 1), (0, 5)):
        span = pl.ds(first, count)
        pltpu.make_async_copy(
            sol.at[span], out.at[span, :, x], own_sem.at[first]
        ).wait()
    whole = out.at[:, :, pl.ds(0, NX - 1)]
    wait(whole, send.at[9])
    wait(whole, recv.at[9])


def solution(mesh):
    def on_device(rhs, upd, diag, lower, vinv, upper, parent, live_count):
        levels, slots, rows, width = rhs.shape
        part = rows // NX
        hbm = pl.BlockSpec(memory_space=pl.ANY)
        dma = pltpu.SemaphoreType.DMA
        pair = slots * width
        tile = (slots * part, width)
        split = (slots, NX, part, width)

        def vmem(*shape, dtype=BF16):
            return pltpu.VMEM(shape, dtype)

        result = pl.pallas_call(
            kernel,
            out_shape=pltpu.VMEM((levels,) + split, BF16),
            in_specs=[hbm] * 8,
            out_specs=hbm,
            scratch_shapes=[
                pltpu.SMEM(parent.shape[::-1], jnp.int32),
                pltpu.SMEM(live_count.shape[::-1], jnp.int32),
                vmem(*diag.shape),
                vmem(*lower.shape),
                vmem(*vinv.shape),
                vmem(*upper.shape),
                vmem(levels - 1, pair, width),
                vmem(levels - 1, pair, width),
                vmem(4, slots, width // NX, width),
                [vmem(SIZES[l] // NC, NC, slots, width // NX, width) for l in range(4)],
                [vmem(n, NX, width // NX, width) for n in (12, 8)],
                [vmem(SIZES[l] // NC, NC, *tile) for l in range(4)],
                pltpu.SMEM((1, 128), jnp.int32),
                pltpu.SMEM((1, 128), jnp.int32),
                pltpu.SMEM((32, 128), jnp.int32),
                vmem(levels, slots, part, width),
                vmem(*split),
                vmem(*split),
                vmem(NX, levels, slots, part, width),
                vmem(levels - 1, *tile, dtype=F32),
                vmem(levels, slots, part, width),
                vmem(levels - 1, pair, width),
                vmem(sum(SIZES[1:4]) + 32, *tile),
                vmem(NX, 4, *tile),
                vmem(16, *tile),
                [vmem(n, *tile) for n in (8, 16, 16, 32)],
                vmem(4, *tile),
                vmem(32, NC, slots, part, width),
                dma((2,)),
                dma((2,)),
                dma((12,)),
                dma((11,)),
                dma((11,)),
                dma((NX - 1,)),
                dma((NX - 1,)),
                dma((2, 4)),
                dma((2, 4)),
                dma((2, 4)),
                dma((2, 4)),
                dma((3,)),
                dma((3,)),
                dma((2,)),
                dma((2,)),
                dma((2, 4)),
                dma((2, 4)),
                dma((levels,)),
            ],
            compiler_params=pltpu.CompilerParams(
                collective_id=0, has_side_effects=True
            ),
        )(
            parent.T,
            live_count.T,
            rhs.reshape(levels, slots, NX, part, width),
            upd.reshape(levels, slots, NX, part, width),
            diag,
            lower,
            vinv,
            upper,
        )
        return result.reshape(rhs.shape)

    return jax.shard_map(
        on_device,
        mesh=mesh,
        in_specs=(
            P(None, "grid", None, None),
            P("gz", None, "grid", None, None),
            P(None, "grid", None, None),
            P(None, "grid", None, None),
            P(None, "grid", None, None),
            P(None, "grid", None, None),
            P(None, "grid"),
            P(None, "grid"),
        ),
        out_specs=P(None, "grid", None, None),
        check_vma=False,
    )
```

```python
import functools

import jax
import jax.numpy as jnp
from jax import lax
from jax.experimental import pallas as pl
from jax.experimental.pallas import tpu as pltpu
from jax.sharding import PartitionSpec as P

MESH = pl.DeviceIdType.MESH
F32 = jnp.float32
BF16 = jnp.bfloat16
NX, NY, NZ, NC = 4, 4, 8, 2
LEVELS = 6
CHIPS_Z = (2, 4, 8, 8, 8)
CHIPS_Y = (1, 1, 1, 2, 4)
SIZES = tuple(NC * a * b for a, b in zip(CHIPS_Z, CHIPS_Y))


def ring(k, n):
    return min(k, n - k)


def offsets(mz, my, cores):
    every = [
        (dy, dz, dc) for dy in range(my) for dz in range(mz) for dc in range(cores)
    ]
    every.sort(key=lambda o: -(ring(o[0], NY) + ring(o[1], NZ)))
    return [o for o in every if o != (0, 0, 0)]


def kernel(
    parent_hbm,
    live_hbm,
    rhs,
    upd,
    diag_hbm,
    lower_hbm,
    vinv_hbm,
    upper_hbm,
    out,
    parent,
    live_count,
    diag,
    lower,
    vinv,
    upper,
    ml,
    top,
    uv_own,
    uv_part,
    tabs,
    picks,
    ftabs,
    ids_own,
    ids_mate,
    ids,
    rhs_own,
    rhs_first,
    upd_first,
    upd_all,
    fv,
    sol,
    chain,
    build,
    build0,
    in0,
    ins,
    mate,
    top_tab,
    mate_send,
    mate_recv,
    load_sem,
    send,
    recv,
    rs_send,
    rs_recv,
    tab_send,
    tab_recv,
    ring_send,
    ring_recv,
    swap_send,
    swap_recv,
    pick_send,
    pick_recv,
    f_send,
    f_recv,
    own_sem,
):
    x = lax.axis_index("gz")
    g = lax.axis_index("grid")
    y, z, c = g // (NZ * NC), lax.rem(g // NC, NZ), lax.rem(g, NC)

    zs = {m: [z // m * m + lax.rem(z + k, m) for k in range(m)] for m in (2, 4, 8)}
    ys = {m: [y // m * m + lax.rem(y + k, m) for k in range(m)] for m in (1, 2, 4)}
    cs = [c, 1 - c]
    xs = [lax.rem(x + k, NX) for k in range(NX)]

    def at(off, mz, my):
        dy, dz, dc = off
        return (ys[my][dy] * NZ + zs[mz][dz]) * NC + cs[dc]

    def remote(src, dst, s, r, gx, gg):
        return pltpu.make_async_remote_copy(
            src_ref=src,
            dst_ref=dst,
            send_sem=s,
            recv_sem=r,
            device_id=(gx, gg),
            device_id_type=MESH,
        )

    def wait(view, sem):
        pltpu.make_async_copy(view, view, sem).wait()

    barrier = pltpu.get_barrier_semaphore()
    near = [(k, g) for k in xs[1:]]
    near += [(k, at(o, 2, 1)) for k in xs for o in offsets(2, 1, 2)]
    near += [(x, at((dy, 0, 0), 8, 4)) for dy in (1, 3)]
    far = [(0, dz, dc) for dz in (1, 2, 6, 7) for dc in (0, 1)]
    for gx, gg in near:
        pl.semaphore_signal(barrier, inc=1, device_id=(gx, gg), device_id_type=MESH)
    for o in far:
        pl.semaphore_signal(
            barrier, inc=1, device_id=(x, at(o, 8, 4)), device_id_type=MESH
        )

    loads = [
        pltpu.make_async_copy(upd.at[0], upd_first, load_sem.at[0]),
        pltpu.make_async_copy(rhs.at[0], rhs_first, load_sem.at[1]),
        pltpu.make_async_copy(diag_hbm.at[0], diag.at[0], load_sem.at[2]),
        pltpu.make_async_copy(lower_hbm.at[0], lower.at[0], load_sem.at[3]),
        pltpu.make_async_copy(vinv_hbm, vinv, load_sem.at[4]),
        pltpu.make_async_copy(upper_hbm, upper, load_sem.at[5]),
        pltpu.make_async_copy(rhs.at[:, :, x], rhs_own, load_sem.at[6]),
        pltpu.make_async_copy(upd.at[:, :, x], upd_all.at[0], load_sem.at[7]),
        pltpu.make_async_copy(
            diag_hbm.at[pl.ds(1, LEVELS - 1)],
            diag.at[pl.ds(1, LEVELS - 1)],
            load_sem.at[8],
        ),
        pltpu.make_async_copy(
            lower_hbm.at[pl.ds(1, LEVELS - 2)],
            lower.at[pl.ds(1, LEVELS - 2)],
            load_sem.at[9],
        ),
    ]
    ints = [
        pltpu.make_async_copy(parent_hbm, parent, load_sem.at[10]),
        pltpu.make_async_copy(live_hbm, live_count, load_sem.at[11]),
    ]
    for copy in ints + loads:
        copy.start()
    for copy in ints:
        copy.wait()
    for l in range(LEVELS - 1):
        for s in range(2):
            ids_own[0, 2 * l + s] = parent[s, l]

    row = lax.broadcasted_iota(jnp.int32, (16, 128), 0)
    slotrow = row // 8

    def spread(v, half):
        rows = lax.broadcasted_iota(jnp.int32, v.shape, 0)
        zero = jnp.zeros_like(v)
        return jnp.concatenate(
            [jnp.where(rows < half, v, zero), jnp.where(rows < half, zero, v)], axis=1
        ).astype(BF16)

    def live_of(l, rows=16):
        slot = lax.broadcasted_iota(jnp.int32, (rows, 128), 0) // (rows // 2)
        return (slot < live_count[0, l]).astype(F32)

    def dot(a, b):
        return jnp.dot(a, b, preferred_element_type=F32)

    def mats(ref, l):
        return ref[l].reshape(256, 128)

    def twice(v):
        return jnp.concatenate([v, v], axis=0)

    def tiles(own, ref, places):
        sums = [own]
        for i, k in enumerate(places):
            tile = ref[k].astype(F32)
            if i < 3:
                sums.append(tile)
            else:
                sums[i % 4] = sums[i % 4] + tile
        while len(sums) > 1:
            sums = [sum(sums[i : i + 2]) for i in range(0, len(sums), 2)]
        return sums[0]

    def target(p, n):
        return lax.rem(p, 2 * n) - slotrow

    def product(a, b, dst, l):
        for s in range(2):
            dst[l, pl.ds(128 * s, 128), :] = dot(a[l, s], b[l, s]).astype(BF16)

    for k in range(4):
        loads[k].wait()
    first = rhs_first[...].astype(F32).reshape(64, 128) * (x == 0).astype(F32)
    first = first - upd_first[...].astype(F32).reshape(64, 128)
    f0 = dot(spread(first, 32), mats(diag, 0)) * live_of(0, 64)
    sent = dot(spread(f0, 32), mats(lower, 0))
    off0 = [(0, 0, 0)] + offsets(2, 1, 2)
    rels = [lax.rem(at(o, 2, 1), 4) for o in off0]
    pa, pb = target(parent[0, 0], 4), target(parent[1, 0], 4)
    for q in range(NX):
        a = twice(sent[8 * q : 8 * q + 8])
        b = twice(sent[32 + 8 * q : 40 + 8 * q])
        zero = jnp.zeros_like(a)
        for k, rel in enumerate(rels):
            build0[q, k] = (
                jnp.where(pa == 2 * rel, a, zero) + jnp.where(pb == 2 * rel, b, zero)
            ).astype(BF16)

    pl.semaphore_wait(barrier, len(near) + len(far))

    for dx in (2, 1, 3, 0):
        for k, o in enumerate(off0):
            if dx or k:
                remote(
                    build0.at[xs[dx], k],
                    in0.at[4 * dx + k],
                    send.at[0],
                    recv.at[0],
                    xs[dx],
                    at(o, 2, 1),
                ).start()
    rs = [
        remote(
            upd.at[:, :, xs[k]],
            upd_all.at[k],
            rs_send.at[k - 1],
            rs_recv.at[k - 1],
            xs[k],
            g,
        )
        for k in range(1, NX)
    ]
    for copy in rs:
        copy.start()

    for k in range(4, 10):
        loads[k].wait()
    partner = at((0, 0, 1), 2, 1)
    part = pl.ds(32 * x, 32)
    up_row = lax.rem(y, 2)
    homes = [lax.rem(z, 2), lax.rem(z, 4), z, up_row * NZ + z]

    for l in (1, 2, 3, 4):
        for s in range(2):
            live = (s < live_count[0, l]).astype(F32)
            quarter = (dot(upper[l, s, part, :], vinv[l, s]) * live).astype(BF16)
            uv_part[l - 1, s] = quarter
            tabs[l - 1][homes[l - 1], c, s] = quarter

    def table_direct(l):
        nz = CHIPS_Z[l - 1]
        for o in offsets(nz, 1, 1):
            remote(
                uv_part.at[l - 1],
                tabs[l - 1].at[homes[l - 1], c],
                tab_send.at[0, l - 1],
                tab_recv.at[0, l - 1],
                x,
                at(o, nz, 1),
            ).start()

    def direct_view(l):
        return tabs[l - 1].at[pl.ds(0, CHIPS_Z[l - 1] - 1), 0]

    def table_ring(step):
        for i, first in ((0, 0), (1, up_row * NZ)):
            tab = tabs[2 + i]
            if step == 3:
                moves = [(z, (0, 4, 0))]
            else:
                moves = [
                    (lax.rem(z + NZ - step, NZ), (0, 1, 0)),
                    (lax.rem(z + step, NZ), (0, 7, 0)),
                ]
            for block, o in moves:
                remote(
                    tab.at[first + block, c] if step else uv_part.at[2 + i],
                    tab.at[first + block, c],
                    ring_send.at[i, step],
                    ring_recv.at[i, step],
                    x,
                    at(o, 8, 1),
                ).start()

    def ring_view(i, step):
        return tabs[2 + i].at[pl.ds(0, 1 if step == 3 else 2), 0]

    def ring_wait(step):
        for i in range(2):
            wait(ring_view(i, step), ring_recv.at[i, step])

    swaps = ((0, 1, 7), (2, 6), (3, 5, 4))

    def rows_swap(step):
        for k in swaps[step]:
            block = tabs[3].at[up_row * NZ + zs[8][k], c]
            remote(
                block,
                block,
                swap_send.at[step],
                swap_recv.at[step],
                x,
                at((1, 0, 0), 8, 2),
            ).start()

    def rows_view(step):
        return tabs[3].at[pl.ds(0, len(swaps[step])), 0]

    def core_swap(l):
        tab = tabs[l - 1]
        remote(
            tab.at[:, c],
            tab.at[:, c],
            tab_send.at[1, l - 1],
            tab_recv.at[1, l - 1],
            x,
            partner,
        ).start()

    def core_view(l):
        return tabs[l - 1].at[:, 0]

    def pick_share(i):
        for k in (2, 1, 3):
            remote(
                picks[i].at[:, x],
                picks[i].at[:, x],
                pick_send.at[i],
                pick_recv.at[i],
                xs[k],
                g,
            ).start()

    def pick_view(i):
        return picks[i].at[:, pl.ds(0, NX - 1)]

    def f_share(l):
        nz, ny = CHIPS_Z[l - 1], CHIPS_Y[l - 1]
        tab = ftabs[l - 1]
        tab[homes[l - 1], c] = fv[l].astype(BF16)
        for o in offsets(nz, ny, 1):
            remote(
                tab.at[homes[l - 1], c],
                tab.at[homes[l - 1], c],
                f_send.at[0, l - 1],
                f_recv.at[0, l - 1],
                x,
                at(o, nz, ny),
            ).start()

    def f_view(l):
        return ftabs[l - 1].at[pl.ds(0, SIZES[l - 1] // NC - 1), 0]

    def f_swap(l):
        wait(f_view(l), f_recv.at[0, l - 1])
        tab = ftabs[l - 1]
        remote(
            tab.at[:, c],
            tab.at[:, c],
            f_send.at[1, l - 1],
            f_recv.at[1, l - 1],
            x,
            partner,
        ).start()

    def f_wait(l):
        wait(ftabs[l - 1].at[:, 0], f_recv.at[1, l - 1])

    def f_tile(l, p):
        return half(ftabs[l - 1][p // 4, lax.rem(p // 2, 2)], p)

    def half(t, p):
        t = t.astype(F32)
        return jnp.where(lax.rem(p, 2) == 0, t[:8], t[8:])

    def forward(l, total):
        fwd = dot(spread(total, 8), mats(diag, l)) * live_of(l)
        fv[l] = dot(spread(fwd, 8), mats(vinv, l)) * live_of(l)

    def base(l):
        total = rhs_own[l].astype(F32).reshape(16, 128)
        for k in range(NX):
            total = total - upd_all[k, l].astype(F32).reshape(16, 128)
        return total

    remote(ids_own, ids_mate, send.at[5], recv.at[5], x, partner).start()
    product(diag, lower, ml, 1)
    table_direct(1)
    table_ring(0)
    for copy in rs:
        copy.wait_recv()
    bases = base(1)
    wait(in0.at[pl.ds(1, 15)], recv.at[0])
    incoming = tiles(build0[x, 0].astype(F32), in0, range(1, 16))

    def mate_terms(l, sent):
        i = 2 * (l - 3)
        mate[i] = sent.astype(BF16)
        remote(
            mate.at[i], mate.at[i + 1], mate_send.at[l - 3], mate_recv.at[l - 3], x, partner
        ).start()
        wait(mate.at[i + 1], mate_recv.at[l - 3])
        theirs = mate[i + 1].astype(F32)
        return [
            (ids_mate[0, 2 * l], theirs[:8]),
            (ids_mate[0, 2 * l + 1], theirs[8:]),
        ]

    def masked(p, v, rel, n):
        return jnp.where(target(p, n) == 2 * rel, twice(v), jnp.zeros((16, 128), F32))

    for l in (1, 2, 3):
        n, mz, my = SIZES[l], CHIPS_Z[l], CHIPS_Y[l]
        total = bases - incoming
        sent = dot(spread(total, 8), ml[l]) * live_of(l)
        terms = [(parent[0, l], sent[:8]), (parent[1, l], sent[8:])]
        if l == 3:
            terms += mate_terms(l, sent)

        def tile(rel):
            return sum(masked(p, v, rel, n) for p, v in terms).astype(BF16)

        offs = offsets(mz, my, 1 if l == 3 else 2)
        goals = [at(o, mz, my) for o in offs]
        start = sum(SIZES[1:l])
        for k, goal in enumerate(goals):
            build[start + k] = tile(lax.rem(goal, n))
        for k, goal in enumerate(goals):
            remote(
                build.at[start + k], ins[l - 1].at[k], send.at[l], recv.at[l], x, goal
            ).start()
        own = tile(lax.rem(g, n)).astype(F32)

        forward(l, total)
        f_share(l)
        if l == 1:
            table_direct(2)
            ring_wait(0)
            table_ring(1)
            rows_swap(0)
            forward(0, base(0))
        if l == 2:
            wait(ids_mate, recv.at[5])
            mine = lax.rem(g, 32)
            for s in range(10):
                ids[mine, s] = ids_own[0, s]
            for o in offsets(8, 1, 2):
                remote(
                    ids_own,
                    ids.at[pl.ds(mine, 1)],
                    send.at[8],
                    recv.at[8],
                    x,
                    at(o, 8, 1),
                ).start()
            ring_wait(1)
            table_ring(2)
            table_ring(3)
            rows_swap(1)
            for j in (1, 2):
                wait(direct_view(j), tab_recv.at[0, j - 1])
                core_swap(j)
        if l == 3:
            wait(ids.at[pl.ds(0, 15)], recv.at[8])
            half_ids = ids.at[pl.ds(16 * up_row, 16)]
            remote(
                half_ids, half_ids, send.at[7], recv.at[7], x, at((1, 0, 0), 8, 2)
            ).start()
            ring_wait(2)
            ring_wait(3)
            rows_swap(2)
            core_swap(3)
        product(diag, lower, ml, l + 1)
        product(upper, vinv, uv_own, l)
        if l == 3:
            for j in (1, 2, 3):
                wait(core_view(j), tab_recv.at[1, j - 1])
            wait(half_ids, recv.at[7])
            chains = []
            for k in range(4):
                for s in range(2):
                    path = {}
                    p = parent[s, k]
                    for j in range(k + 1, 5):
                        n = SIZES[j - 1]
                        path[j] = lax.rem(p, 2 * n)
                        p = ids[
                            lax.rem(path[j] // 2, n) + (g // n * n - g // 32 * 32),
                            2 * j + lax.rem(path[j], 2),
                        ]
                    path[5] = lax.rem(p, 128)
                    chains.append(path)
            places = {}
            for k in range(3):
                for s in range(2):
                    for j in range(k + 1, 4):
                        p = chains[2 * k + s][j]
                        places[k, s, j] = len(places)
                        picks[0][places[k, s, j], x] = tabs[j - 1][
                            p // 4, lax.rem(p // 2, 2), lax.rem(p, 2)
                        ]
            pick_share(0)
        bases = base(l + 1)
        wait(ins[l - 1].at[pl.ds(0, len(goals))], recv.at[l])
        incoming = tiles(own, ins[l - 1], range(len(goals)))

    total = bases - incoming
    sent = dot(spread(total, 8), ml[4]) * live_of(4)
    terms = [(parent[0, 4], sent[:8]), (parent[1, 4], sent[8:])]
    offs = offsets(8, 4, 1)
    goals = [at(o, 8, 4) for o in offs]
    bases = base(5)
    terms += mate_terms(4, sent)

    def tile4(goal):
        return sum(masked(p, v, goal, 64) for p, v in terms).astype(BF16)

    start = sum(SIZES[1:4])
    for k, goal in enumerate(goals):
        build[start + k] = tile4(goal)
    for k, goal in enumerate(goals):
        remote(
            build.at[start + k], ins[3].at[k], send.at[4], recv.at[4], x, goal
        ).start()
    own = tile4(g).astype(F32)
    for j in (1, 2, 3):
        f_swap(j)
    for step in range(3):
        wait(rows_view(step), swap_recv.at[step])
    core_swap(4)
    forward(4, total)
    f_share(4)
    product(upper, vinv, uv_own, 4)
    product(upper, vinv, uv_own, 0)
    for s in range(2):
        top[pl.ds(128 * s, 128), :] = dot(diag[5, s], vinv[5, s]).astype(BF16)
    wait(core_view(4), tab_recv.at[1, 3])
    for k in range(4):
        for s in range(2):
            p = chains[2 * k + s][4]
            picks[1][2 * k + s, x] = tabs[3][p // 4, lax.rem(p // 2, 2), lax.rem(p, 2)]
    pick_share(1)

    wait(pick_view(0), pick_recv.at[0])
    for j in (1, 2, 3):
        f_wait(j)
    for k in range(4):
        consts = []
        for s in range(2):
            path = chains[2 * k + s]
            m = const = None
            for j in range(3, k - 1, -1):
                if j == k:
                    u = uv_own[k, pl.ds(128 * s, 128), :]
                    f = fv[k, pl.ds(8 * s, 8), :]
                else:
                    u = picks[0][places[k, s, j]].reshape(128, 128)
                    f = f_tile(j, path[j])
                if m is None:
                    m, const = u, f
                else:
                    const = f - dot(const.astype(BF16), u)
                    m = dot(m, u).astype(BF16)
            chain[k, pl.ds(128 * s, 128), :] = m
            consts.append(const)
        fv[k] = jnp.concatenate(consts, axis=0)
    wait(ins[3].at[pl.ds(0, 31)], recv.at[4])
    incoming = tiles(own, ins[3], range(31))

    answer = (dot(spread(bases - incoming, 8), top[...]) * live_of(5)).astype(BF16)
    sol[5] = answer.reshape(2, 8, 128)

    def share(first, count):
        span = pl.ds(first, count)
        for k in (2, 1, 3):
            remote(
                sol.at[span], out.at[span, :, x], send.at[9], recv.at[9], xs[k], g
            ).start()
        pltpu.make_async_copy(
            sol.at[span], out.at[span, :, x], own_sem.at[first]
        ).start()

    chip = y * NZ + z
    for o in offs:
        remote(
            sol.at[5], top_tab.at[chip, c], send.at[6], recv.at[6], x, at(o, 8, 4)
        ).start()
    top_tab[chip, c] = sol[5]
    share(5, 1)

    f_swap(4)
    wait(pick_view(1), pick_recv.at[1])
    f_wait(4)
    for k in range(4):
        sign = 1 if k % 2 == 0 else -1
        ends = [chains[2 * k + s][4] for s in range(2)]
        f = jnp.concatenate([f_tile(4, p) for p in ends], axis=0)
        fv[k] = fv[k] + sign * dot(spread(f, 8), chain[k])
        for s in range(2):
            span = pl.ds(128 * s, 128)
            u = picks[1][2 * k + s].reshape(128, 128)
            chain[k, span, :] = dot(u, chain[k, span, :]).astype(BF16)
    for s in range(2):
        chain[4, pl.ds(128 * s, 128), :] = uv_own[4, pl.ds(128 * s, 128), :]

    wait(top_tab.at[pl.ds(0, 31), 0], recv.at[6])
    remote(
        top_tab.at[:, c], top_tab.at[:, c], send.at[10], recv.at[10], x, partner
    ).start()
    wait(top_tab.at[:, 0], recv.at[10])
    for k in range(5):
        if k < 4:
            ends = [chains[2 * k + s][5] for s in range(2)]
        else:
            ends = [lax.rem(parent[s, 4], 128) for s in range(2)]
        above = jnp.concatenate(
            [
                top_tab[p // 4, lax.rem(p // 2, 2), lax.rem(p, 2)].astype(F32)
                for p in ends
            ],
            axis=0,
        )
        low = dot(spread(above, 8), chain[k])
        value = fv[k] + low if k % 2 == 1 else fv[k] - low
        sol[k] = (value * live_of(k)).astype(BF16).reshape(2, 8, 128)
    share(0, 5)

    wait(in0.at[pl.ds(1, 15)], send.at[0])
    for copy in rs:
        copy.wait_send()
    for l in (1, 2):
        wait(ins[l - 1].at[pl.ds(0, SIZES[l] - 1)], send.at[l])
        wait(direct_view(l), tab_send.at[0, l - 1])
    wait(ins[2].at[pl.ds(0, 15)], send.at[3])
    for i in range(2):
        wait(mate.at[2 * i], mate_send.at[i])
    for step in range(4):
        for i in range(2):
            wait(ring_view(i, step), ring_send.at[i, step])
    for step in range(3):
        wait(rows_view(step), swap_send.at[step])
    for l in (1, 2, 3, 4):
        wait(core_view(l), tab_send.at[1, l - 1])
        wait(f_view(l), f_send.at[0, l - 1])
        wait(ftabs[l - 1].at[:, 0], f_send.at[1, l - 1])
    for i in range(2):
        wait(pick_view(i), pick_send.at[i])
    wait(ins[3].at[pl.ds(0, 31)], send.at[4])
    wait(ids_own, send.at[5])
    wait(top_tab.at[pl.ds(0, 31), 0], send.at[6])
    wait(half_ids, send.at[7])
    wait(ids.at[pl.ds(0, 15)], send.at[8])
    wait(top_tab.at[:, 0], send.at[10])
    for first, count in ((5, 1), (0, 5)):
        span = pl.ds(first, count)
        pltpu.make_async_copy(
            sol.at[span], out.at[span, :, x], own_sem.at[first]
        ).wait()
    whole = out.at[:, :, pl.ds(0, NX - 1)]
    wait(whole, send.at[9])
    wait(whole, recv.at[9])


def solution(mesh):
    def on_device(rhs, upd, diag, lower, vinv, upper, parent, live_count):
        levels, slots, rows, width = rhs.shape
        part = rows // NX
        hbm = pl.BlockSpec(memory_space=pl.ANY)
        dma = pltpu.SemaphoreType.DMA
        pair = slots * width
        tile = (slots * part, width)
        split = (slots, NX, part, width)

        def vmem(*shape, dtype=BF16):
            return pltpu.VMEM(shape, dtype)

        result = pl.pallas_call(
            kernel,
            out_shape=pltpu.VMEM((levels,) + split, BF16),
            in_specs=[hbm] * 8,
            out_specs=hbm,
            scratch_shapes=[
                pltpu.SMEM(parent.shape[::-1], jnp.int32),
                pltpu.SMEM(live_count.shape[::-1], jnp.int32),
                vmem(*diag.shape),
                vmem(*lower.shape),
                vmem(*vinv.shape),
                vmem(*upper.shape),
                vmem(levels - 1, pair, width),
                vmem(pair, width),
                vmem(levels - 1, pair, width),
                vmem(4, slots, width // NX, width),
                [vmem(SIZES[l] // NC, NC, slots, width // NX, width) for l in range(4)],
                [vmem(n, NX, width // NX, width) for n in (12, 8)],
                [vmem(SIZES[l] // NC, NC, *tile) for l in range(4)],
                pltpu.SMEM((1, 128), jnp.int32),
                pltpu.SMEM((1, 128), jnp.int32),
                pltpu.SMEM((32, 128), jnp.int32),
                vmem(levels, slots, part, width),
                vmem(*split),
                vmem(*split),
                vmem(NX, levels, slots, part, width),
                vmem(levels - 1, *tile, dtype=F32),
                vmem(levels, slots, part, width),
                vmem(levels - 1, pair, width),
                vmem(sum(SIZES[1:4]) + 32, *tile),
                vmem(NX, 4, *tile),
                vmem(16, *tile),
                [vmem(n, *tile) for n in (8, 16, 16, 32)],
                vmem(4, *tile),
                vmem(32, NC, slots, part, width),
                dma((2,)),
                dma((2,)),
                dma((12,)),
                dma((11,)),
                dma((11,)),
                dma((NX - 1,)),
                dma((NX - 1,)),
                dma((2, 4)),
                dma((2, 4)),
                dma((2, 4)),
                dma((2, 4)),
                dma((3,)),
                dma((3,)),
                dma((2,)),
                dma((2,)),
                dma((2, 4)),
                dma((2, 4)),
                dma((levels,)),
            ],
            compiler_params=pltpu.CompilerParams(
                collective_id=0, has_side_effects=True
            ),
        )(
            parent.T,
            live_count.T,
            rhs.reshape(levels, slots, NX, part, width),
            upd.reshape(levels, slots, NX, part, width),
            diag,
            lower,
            vinv,
            upper,
        )
        return result.reshape(rhs.shape)

    return jax.shard_map(
        on_device,
        mesh=mesh,
        in_specs=(
            P(None, "grid", None, None),
            P("gz", None, "grid", None, None),
            P(None, "grid", None, None),
            P(None, "grid", None, None),
            P(None, "grid", None, None),
            P(None, "grid", None, None),
            P(None, "grid"),
            P(None, "grid"),
        ),
        out_specs=P(None, "grid", None, None),
        check_vma=False,
    )
```
